32 devices in a mesh: pair: 8 (over y, x, core), aux: 4 (over z).
Axes of the slice: x: 2, y: 2, z: 4, core: 2. Of those that a mesh axis runs over, the one named last changes fastest.
Arguments:
- three_center: float32 [2048, 8192], P('aux', 'pair'), may hold values from -0.0625 to 0.0625
- densities: float32 [8192, 512], P(('pair', 'aux')), may hold values from -6 to 6
- screen_mask: int32 [32, 128], P('aux', 'pair'), may hold values 0 or 1
- diag_inverse: float32 [2048, 512], P('aux'), as said below
- sub_factor: float32 [2048, 512], P('aux'), as said below
Outputs:
- response: float32 [8192, 512], P(('pair', 'aux'))
The draws below stay inside these ranges and needn't reach their ends.
Inputs may be any that keep to these rules, and one draw needn't show every extreme that they name: `diag_inverse`: each block of 512 rows is lower triangular; its diagonal lies in 0.75 to 1.3 and its entries below the diagonal within plus or minus 2 / sqrt(512). `sub_factor`: block 0 is not used; entries lie within plus or minus 3.4 / sqrt(512).
All inputs are finite; a program needn't handle non-finite values. No bound on the sum of `screen_mask` on one device may be relied on, other than what follows from the above.
Results may differ from the reference program's by a relative error of at most 0.0003.
Values sent between devices are 32-bit elements; how exact they have to be, the bound alone decides.
No kernel may reach another device: no remote copies, remote signals or barrier semaphores. Data moves between devices by JAX's collectives and lax.ppermute only.
A program may use at most 192 MiB of HBM per device.

```python
import math
import jax
import jax.numpy as jnp
from jax import lax

AUX_DEV = 512
NV = 512
SCREEN = 64
NAUX = 2048
NPAIR = 8192


def draw_diag_inverse(key, part):
    first, second = jax.random.split(jax.random.fold_in(key, 17), 2)
    full_shape = (NAUX, AUX_DEV)
    row_index = lax.broadcasted_iota(jnp.int32, full_shape, 0) % AUX_DEV
    col_index = lax.broadcasted_iota(jnp.int32, full_shape, 1)
    spread = 0.5 / math.sqrt(AUX_DEV)
    below = jax.random.truncated_normal(first, -4.0, 4.0, full_shape, jnp.float32) * spread
    diagonal = jax.random.uniform(second, full_shape, jnp.float32, 0.8, 1.25)
    return jnp.where(row_index > col_index, below, jnp.where(row_index == col_index, diagonal, 0.0)).astype(jnp.float32)


def draw_sub_factor(key, part):
    first = jax.random.fold_in(key, 29)
    full_shape = (NAUX, AUX_DEV)
    spread = 0.85 / math.sqrt(AUX_DEV)
    values = jax.random.truncated_normal(first, -4.0, 4.0, full_shape, jnp.float32) * spread
    return values.astype(jnp.float32)


def set_ends(result, key, low, high):
    spot = [jax.random.randint(jax.random.fold_in(key, axis), (), 0, length) for axis, length in enumerate(result.shape)]
    main_axis = result.shape.index(max(result.shape))
    beside = spot[:main_axis] + [(spot[main_axis] + 1) % result.shape[main_axis]] + spot[main_axis + 1:]
    return result.at[tuple(spot)].set(low).at[tuple(beside)].set(high)


def levels(rng, dims, cuts, smallest, high):
    factor_of, own = 1.0, jax.random.fold_in(rng, 6)
    for position, shards_of in cuts:
        draws = jnp.exp(jax.random.uniform(jax.random.fold_in(own, position), (shards_of,), jnp.float32, smallest / len(cuts), high / len(cuts)))
        factor_of = factor_of * jnp.repeat(draws, dims[position] // shards_of).reshape([-1 if axis == position else 1 for axis in range(len(dims))])
    return factor_of


def centred(key, dims, scale, limit, pieces=(), dtype=jnp.bfloat16):
    result = jax.random.normal(key, dims, jnp.float32) * scale
    if len(pieces) > 0:
        result = levels(key, dims, pieces, -0.22, 0.18) * result
    return jnp.clip(result, min=-limit, max=limit).astype(dtype)


def setup_inputs(seed: int = 0) -> dict:
    keys = jax.random.split(jax.random.key(seed), 6)
    return {
        "three_center": centred(keys[0], (NAUX, NPAIR), NPAIR ** -0.5, 0.0625, ((0, 4), (1, 8)), jnp.float32),
        "densities": centred(keys[1], (NPAIR, NV), 1.0, 6.0, ((0, 32),), jnp.float32),
        "screen_mask": set_ends((jax.random.randint(keys[2], (NAUX // SCREEN, NPAIR // SCREEN), 0, 4) < 3).astype(jnp.int32), jax.random.fold_in(keys[2], 1), 0, 1),
        "diag_inverse": draw_diag_inverse(jax.random.fold_in(keys[5], 71), 0),
        "sub_factor": draw_sub_factor(jax.random.fold_in(keys[5], 71), 0),
    }


def screen_block(block, screen_mask):
    aux_blocks, pair_blocks = screen_mask.shape
    aux_size = block.shape[0] // aux_blocks
    pair_size = block.shape[1] // pair_blocks
    shaped = block.reshape(aux_blocks, aux_size, pair_blocks, pair_size)
    shaped = shaped * screen_mask.astype(jnp.float32)[:, None, :, None]
    return shaped.reshape(block.shape)


def product(left, right):
    return jnp.dot(left, right, precision=lax.Precision.HIGHEST, preferred_element_type=jnp.float32)


def reference(three_center, densities, screen_mask, diag_inverse, sub_factor):
    screened = screen_block(three_center, screen_mask)
    gamma = product(screened, densities)
    count_blocks = NAUX // AUX_DEV
    previous = jnp.zeros((AUX_DEV, NV), jnp.float32)
    solved = []
    for block_index in range(count_blocks):
        first_row = block_index * AUX_DEV
        inverse = diag_inverse[first_row:first_row + AUX_DEV]
        lower = sub_factor[first_row:first_row + AUX_DEV]
        gamma_block = gamma[first_row:first_row + AUX_DEV]
        previous = product(inverse, gamma_block - product(lower, previous))
        solved.append(previous)
    carried = jnp.zeros((AUX_DEV, NV), jnp.float32)
    coefficients = [None] * count_blocks
    for block_index in range(count_blocks - 1, -1, -1):
        first_row = block_index * AUX_DEV
        inverse = diag_inverse[first_row:first_row + AUX_DEV]
        lower = sub_factor[first_row:first_row + AUX_DEV]
        current = product(inverse.T, solved[block_index] - carried)
        coefficients[block_index] = current
        carried = product(lower.T, current)
    coeff_all = jnp.concatenate(coefficients, axis=0)
    return lax.dot_general(screened, coeff_all, (((0,), (0,)), ((), ())), precision=lax.Precision.HIGHEST, preferred_element_type=jnp.float32)
```

```python
import jax
import jax.numpy as jnp
from jax import lax
from jax.sharding import PartitionSpec as P


def from_behind(array, axis, by):
    count = lax.axis_size(axis)
    pairs = [(i, i + by) for i in range(count) if 0 <= i + by < count]
    return lax.ppermute(array, axis, pairs)


def swap(array, axis, bit):
    count = lax.axis_size(axis)
    return lax.ppermute(array, axis, [(i, i ^ bit) for i in range(count)])


def screen_block(block, screen_mask):
    aux_blocks, pair_blocks = screen_mask.shape
    aux_size = block.shape[0] // aux_blocks
    pair_size = block.shape[1] // pair_blocks
    shaped = block.reshape(aux_blocks, aux_size, pair_blocks, pair_size)
    shaped = shaped * screen_mask.astype(jnp.float32)[:, None, :, None]
    return shaped.reshape(block.shape)


def product(left, right):
    return jnp.dot(left, right, precision=lax.Precision.HIGH, preferred_element_type=jnp.float32)


def contract_first(left, right):
    return lax.dot_general(
        left,
        right,
        (((0,), (0,)), ((), ())),
        precision=lax.Precision.HIGH,
        preferred_element_type=jnp.float32,
    )


def reduce_scatter_columns(partial, axis):
    index = lax.axis_index(axis)
    count = lax.axis_size(axis)
    current = partial
    bit = 1
    while bit < count:
        width = current.shape[1] // 2
        low, high = current[:, :width], current[:, width:]
        upper = (index // bit) % 2 == 1
        send = jnp.where(upper, low, high)
        keep = jnp.where(upper, high, low)
        current = keep + swap(send, axis, bit)
        bit *= 2
    return current


def all_gather_columns(share, axis):
    index = lax.axis_index(axis)
    count = lax.axis_size(axis)
    current = share
    bit = count // 2
    while bit >= 1:
        other = swap(current, axis, bit)
        upper = (index // bit) % 2 == 1
        current = jnp.where(
            upper,
            jnp.concatenate([other, current], axis=1),
            jnp.concatenate([current, other], axis=1),
        )
        bit //= 2
    return current


def gamma_over_aux(screened, densities):
    count = lax.axis_size("aux")
    index = lax.axis_index("aux")
    rows = densities.shape[0]

    def columns(block):
        start = jnp.clip(block, 0, count - 1) * rows
        return lax.dynamic_slice_in_dim(screened, start, rows, axis=1)

    gamma = product(columns(index), densities)
    from_left, from_right = densities, densities
    for step in range(count - 1):
        from_left = from_behind(from_left, "aux", 1)
        from_right = from_behind(from_right, "aux", -1)
        gamma = gamma + product(columns(index - 1 - step), from_left)
        gamma = gamma + product(columns(index + 1 + step), from_right)
    return gamma


def per_device(three_center, densities, screen_mask, diag_inverse, sub_factor):
    screened = screen_block(three_center, screen_mask)
    gamma_partial = gamma_over_aux(screened, densities)
    right_side = reduce_scatter_columns(gamma_partial, "pair")
    transfer = -product(diag_inverse, sub_factor)
    driving = product(diag_inverse, right_side)
    chain_length = lax.axis_size("aux")

    incoming = from_behind(driving, "aux", 1)
    for _ in range(chain_length - 2):
        incoming = from_behind(product(transfer, incoming) + driving, "aux", 1)
    solved = product(transfer, incoming) + driving
    source = product(sub_factor.T, product(diag_inverse.T, solved))
    back_map = transfer.T

    arriving = from_behind(source, "aux", -1)
    for _ in range(chain_length - 2):
        arriving = from_behind(product(back_map, arriving) + source, "aux", -1)
    coefficients = product(diag_inverse.T, solved - arriving)
    coeff_full = all_gather_columns(coefficients, "pair")
    partial = contract_first(screened, coeff_full)
    count = lax.axis_size("aux")
    exchanged = lax.all_to_all(partial, "aux", 0, 0, tiled=True)
    return exchanged.reshape(count, partial.shape[0] // count, -1).sum(axis=0)


def solution(mesh):
    return jax.shard_map(
        per_device,
        mesh=mesh,
        in_specs=(
            P("aux", "pair"),
            P(("pair", "aux"), None),
            P("aux", "pair"),
            P("aux", None),
            P("aux", None),
        ),
        out_specs=P(("pair", "aux"), None),
        check_vma=False,
    )
```

```python
import jax
import jax.numpy as jnp
from jax import lax
from jax.sharding import PartitionSpec as P


def from_behind(array, axis, by):
    count = lax.axis_size(axis)
    pairs = [(i, i + by) for i in range(count) if 0 <= i + by < count]
    return lax.ppermute(array, axis, pairs)


def swap(array, axis, bit):
    count = lax.axis_size(axis)
    return lax.ppermute(array, axis, [(i, i ^ bit) for i in range(count)])


def screen_block(block, screen_mask):
    aux_blocks, pair_blocks = screen_mask.shape
    aux_size = block.shape[0] // aux_blocks
    pair_size = block.shape[1] // pair_blocks
    expanded = jnp.repeat(jnp.repeat(screen_mask.astype(jnp.float32), aux_size, 0), pair_size, 1)
    return block * expanded


def product(left, right):
    return jnp.dot(left, right, precision=lax.Precision.HIGH, preferred_element_type=jnp.float32)


def contract_first(left, right):
    return lax.dot_general(
        left,
        right,
        (((0,), (0,)), ((), ())),
        precision=lax.Precision.HIGH,
        preferred_element_type=jnp.float32,
    )


def reduce_scatter_columns(partial, axis):
    index = lax.axis_index(axis)
    count = lax.axis_size(axis)
    current = partial
    bit = 1
    while bit < count:
        width = current.shape[1] // 2
        low, high = current[:, :width], current[:, width:]
        upper = (index // bit) % 2 == 1
        send = jnp.where(upper, low, high)
        keep = jnp.where(upper, high, low)
        current = keep + swap(send, axis, bit)
        bit *= 2
    return current


def all_gather_columns(share, axis):
    index = lax.axis_index(axis)
    count = lax.axis_size(axis)
    current = share
    bit = count // 2
    while bit >= 1:
        other = swap(current, axis, bit)
        upper = (index // bit) % 2 == 1
        current = jnp.where(
            upper,
            jnp.concatenate([other, current], axis=1),
            jnp.concatenate([current, other], axis=1),
        )
        bit //= 2
    return current


def gamma_over_aux(screened, densities):
    count = lax.axis_size("aux")
    index = lax.axis_index("aux")
    rows = densities.shape[0]

    def columns(block):
        start = jnp.clip(block, 0, count - 1) * rows
        return lax.dynamic_slice_in_dim(screened, start, rows, axis=1)

    gamma = product(columns(index), densities)
    from_left, from_right = densities, densities
    for step in range(count - 1):
        from_left = from_behind(from_left, "aux", 1)
        from_right = from_behind(from_right, "aux", -1)
        gamma = gamma + product(columns(index - 1 - step), from_left)
        gamma = gamma + product(columns(index + 1 + step), from_right)
    return gamma


def reduce_over_aux(partial):
    count = lax.axis_size("aux")
    index = lax.axis_index("aux")
    rows = partial.shape[0] // count

    def block(owner):
        start = jnp.clip(owner, 0, count - 1) * rows
        return lax.dynamic_slice_in_dim(partial, start, rows, axis=0)

    to_right = jnp.zeros((rows, partial.shape[1]), partial.dtype)
    to_left = jnp.zeros((rows, partial.shape[1]), partial.dtype)
    for step in range(count - 1):
        to_right = from_behind(to_right + block(index + count - 1 - step), "aux", 1)
        to_left = from_behind(to_left + block(index - (count - 1) + step), "aux", -1)
    return to_right + to_left + block(index)


def solve(right_side, transfer, diag_inverse, sub_factor):
    driving = product(diag_inverse, right_side)
    chain_length = lax.axis_size("aux")
    incoming = from_behind(driving, "aux", 1)
    for _ in range(chain_length - 2):
        incoming = from_behind(product(transfer, incoming) + driving, "aux", 1)
    solved = product(transfer, incoming) + driving
    source = product(sub_factor.T, product(diag_inverse.T, solved))
    back_map = transfer.T
    arriving = from_behind(source, "aux", -1)
    for _ in range(chain_length - 2):
        arriving = from_behind(product(back_map, arriving) + source, "aux", -1)
    return product(diag_inverse.T, solved - arriving)


SLICES = 2


def per_device(three_center, densities, screen_mask, diag_inverse, sub_factor):
    screened = screen_block(three_center, screen_mask)
    transfer = -product(diag_inverse, sub_factor)
    width = densities.shape[1] // SLICES
    results = []
    for part in range(SLICES):
        dens_part = densities[:, part * width:(part + 1) * width]
        gamma_partial = gamma_over_aux(screened, dens_part)
        right_side = reduce_scatter_columns(gamma_partial, "pair")
        coefficients = solve(right_side, transfer, diag_inverse, sub_factor)
        coeff_full = all_gather_columns(coefficients, "pair")
        partial = contract_first(screened, coeff_full)
        results.append(reduce_over_aux(partial))
    return jnp.concatenate(results, axis=1)


def solution(mesh):
    return jax.shard_map(
        per_device,
        mesh=mesh,
        in_specs=(
            P("aux", "pair"),
            P(("pair", "aux"), None),
            P("aux", "pair"),
            P("aux", None),
            P("aux", None),
        ),
        out_specs=P(("pair", "aux"), None),
        check_vma=False,
    )
```

```python
import jax
import jax.numpy as jnp
from jax import lax
from jax.sharding import PartitionSpec as P


def from_behind(array, axis, by):
    count = lax.axis_size(axis)
    pairs = [(i, i + by) for i in range(count) if 0 <= i + by < count]
    return lax.ppermute(array, axis, pairs)


def swap(array, axis, bit):
    count = lax.axis_size(axis)
    return lax.ppermute(array, axis, [(i, i ^ bit) for i in range(count)])


def screen_block(block, screen_mask):
    aux_blocks, pair_blocks = screen_mask.shape
    aux_size = block.shape[0] // aux_blocks
    pair_size = block.shape[1] // pair_blocks
    expanded = jnp.repeat(jnp.repeat(screen_mask.astype(jnp.float32), aux_size, 0), pair_size, 1)
    return block * expanded


def product(left, right):
    return jnp.dot(left, right, precision=lax.Precision.HIGH, preferred_element_type=jnp.float32)


def contract_first(left, right):
    return lax.dot_general(
        left,
        right,
        (((0,), (0,)), ((), ())),
        precision=lax.Precision.HIGH,
        preferred_element_type=jnp.float32,
    )


def reduce_scatter_columns(partial, axis):
    index = lax.axis_index(axis)
    count = lax.axis_size(axis)
    current = partial
    bit = 1
    while bit < count:
        width = current.shape[1] // 2
        low, high = current[:, :width], current[:, width:]
        upper = (index // bit) % 2 == 1
        send = jnp.where(upper, low, high)
        keep = jnp.where(upper, high, low)
        current = keep + swap(send, axis, bit)
        bit *= 2
    return current


def all_gather_columns(share, axis):
    index = lax.axis_index(axis)
    count = lax.axis_size(axis)
    current = share
    bit = count // 2
    while bit >= 1:
        other = swap(current, axis, bit)
        upper = (index // bit) % 2 == 1
        current = jnp.where(
            upper,
            jnp.concatenate([other, current], axis=1),
            jnp.concatenate([current, other], axis=1),
        )
        bit //= 2
    return current


def gamma_over_aux(screened, densities):
    count = lax.axis_size("aux")
    index = lax.axis_index("aux")
    rows = densities.shape[0]

    def columns(block):
        start = jnp.clip(block, 0, count - 1) * rows
        return lax.dynamic_slice_in_dim(screened, start, rows, axis=1)

    gamma = product(columns(index), densities)
    from_left, from_right = densities, densities
    for step in range(count - 1):
        from_left = from_behind(from_left, "aux", 1)
        from_right = from_behind(from_right, "aux", -1)
        gamma = gamma + product(columns(index - 1 - step), from_left)
        gamma = gamma + product(columns(index + 1 + step), from_right)
    return gamma


def reduce_over_aux(partial):
    count = lax.axis_size("aux")
    index = lax.axis_index("aux")
    rows = partial.shape[0] // count

    def block(owner):
        start = jnp.clip(owner, 0, count - 1) * rows
        return lax.dynamic_slice_in_dim(partial, start, rows, axis=0)

    to_right = jnp.zeros((rows, partial.shape[1]), partial.dtype)
    to_left = jnp.zeros((rows, partial.shape[1]), partial.dtype)
    for step in range(count - 1):
        to_right = from_behind(to_right + block(index + count - 1 - step), "aux", 1)
        to_left = from_behind(to_left + block(index - (count - 1) + step), "aux", -1)
    return to_right + to_left + block(index)


def solve(right_side, transfer, diag_inverse, sub_factor):
    driving = product(diag_inverse, right_side)
    chain_length = lax.axis_size("aux")
    incoming = from_behind(driving, "aux", 1)
    for _ in range(chain_length - 2):
        incoming = from_behind(product(transfer, incoming) + driving, "aux", 1)
    solved = product(transfer, incoming) + driving
    source = product(sub_factor.T, product(diag_inverse.T, solved))
    back_map = transfer.T
    arriving = from_behind(source, "aux", -1)
    for _ in range(chain_length - 2):
        arriving = from_behind(product(back_map, arriving) + source, "aux", -1)
    return product(diag_inverse.T, solved - arriving)


SLICES = 2


def per_device(three_center, densities, screen_mask, diag_inverse, sub_factor):
    screened = screen_block(three_center, screen_mask)
    transfer = -product(diag_inverse, sub_factor)
    width = densities.shape[1] // SLICES
    results = []
    for part in range(SLICES):
        dens_part = densities[:, part * width:(part + 1) * width]
        dens_full = lax.all_gather(dens_part, "aux", axis=0, tiled=True)
        gamma_partial = product(screened, dens_full)
        right_side = reduce_scatter_columns(gamma_partial, "pair")
        coefficients = solve(right_side, transfer, diag_inverse, sub_factor)
        coeff_full = all_gather_columns(coefficients, "pair")
        partial = contract_first(screened, coeff_full)
        results.append(lax.psum_scatter(partial, "aux", scatter_dimension=0, tiled=True))
    return jnp.concatenate(results, axis=1)


def solution(mesh):
    return jax.shard_map(
        per_device,
        mesh=mesh,
        in_specs=(
            P("aux", "pair"),
            P(("pair", "aux"), None),
            P("aux", "pair"),
            P("aux", None),
            P("aux", None),
        ),
        out_specs=P(("pair", "aux"), None),
        check_vma=False,
    )
```

```python
import jax
import jax.numpy as jnp
from jax import lax
from jax.sharding import PartitionSpec as P


def from_behind(array, axis, by):
    count = lax.axis_size(axis)
    pairs = [(i, i + by) for i in range(count) if 0 <= i + by < count]
    return lax.ppermute(array, axis, pairs)


def swap(array, axis, bit):
    count = lax.axis_size(axis)
    return lax.ppermute(array, axis, [(i, i ^ bit) for i in range(count)])


def screen_block(block, screen_mask):
    aux_blocks, pair_blocks = screen_mask.shape
    aux_size = block.shape[0] // aux_blocks
    pair_size = block.shape[1] // pair_blocks
    expanded = jnp.repeat(jnp.repeat(screen_mask.astype(jnp.float32), aux_size, 0), pair_size, 1)
    return block * expanded


def product(left, right):
    return jnp.dot(left, right, precision=lax.Precision.HIGH, preferred_element_type=jnp.float32)


def contract_first(left, right):
    return lax.dot_general(
        left,
        right,
        (((0,), (0,)), ((), ())),
        precision=lax.Precision.HIGH,
        preferred_element_type=jnp.float32,
    )


def reduce_scatter_columns(partial, axis):
    index = lax.axis_index(axis)
    count = lax.axis_size(axis)
    current = partial
    bit = 1
    while bit < count:
        width = current.shape[1] // 2
        low, high = current[:, :width], current[:, width:]
        upper = (index // bit) % 2 == 1
        send = jnp.where(upper, low, high)
        keep = jnp.where(upper, high, low)
        current = keep + swap(send, axis, bit)
        bit *= 2
    return current


def all_gather_columns(share, axis):
    index = lax.axis_index(axis)
    count = lax.axis_size(axis)
    current = share
    bit = count // 2
    while bit >= 1:
        other = swap(current, axis, bit)
        upper = (index // bit) % 2 == 1
        current = jnp.where(
            upper,
            jnp.concatenate([other, current], axis=1),
            jnp.concatenate([current, other], axis=1),
        )
        bit //= 2
    return current


def gamma_over_aux(screened, densities):
    count = lax.axis_size("aux")
    index = lax.axis_index("aux")
    rows = densities.shape[0]

    def columns(block):
        start = jnp.clip(block, 0, count - 1) * rows
        return lax.dynamic_slice_in_dim(screened, start, rows, axis=1)

    gamma = product(columns(index), densities)
    from_left, from_right = densities, densities
    for step in range(count - 1):
        from_left = from_behind(from_left, "aux", 1)
        from_right = from_behind(from_right, "aux", -1)
        gamma = gamma + product(columns(index - 1 - step), from_left)
        gamma = gamma + product(columns(index + 1 + step), from_right)
    return gamma


def reduce_over_aux(partial):
    count = lax.axis_size("aux")
    index = lax.axis_index("aux")
    rows = partial.shape[0] // count

    def block(owner):
        start = jnp.clip(owner, 0, count - 1) * rows
        return lax.dynamic_slice_in_dim(partial, start, rows, axis=0)

    to_right = jnp.zeros((rows, partial.shape[1]), partial.dtype)
    to_left = jnp.zeros((rows, partial.shape[1]), partial.dtype)
    for step in range(count - 1):
        to_right = from_behind(to_right + block(index + count - 1 - step), "aux", 1)
        to_left = from_behind(to_left + block(index - (count - 1) + step), "aux", -1)
    return to_right + to_left + block(index)


def solve(right_side, transfer, diag_inverse, sub_factor):
    driving = product(diag_inverse, right_side)
    chain_length = lax.axis_size("aux")
    incoming = from_behind(driving, "aux", 1)
    for _ in range(chain_length - 2):
        incoming = from_behind(product(transfer, incoming) + driving, "aux", 1)
    solved = product(transfer, incoming) + driving
    source = product(sub_factor.T, product(diag_inverse.T, solved))
    back_map = transfer.T
    arriving = from_behind(source, "aux", -1)
    for _ in range(chain_length - 2):
        arriving = from_behind(product(back_map, arriving) + source, "aux", -1)
    return product(diag_inverse.T, solved - arriving)


SLICES = 2


def per_device(three_center, densities, screen_mask, diag_inverse, sub_factor):
    screened = screen_block(three_center, screen_mask)
    transfer = -product(diag_inverse, sub_factor)
    width = densities.shape[1] // SLICES
    results = []
    for part in range(SLICES):
        dens_part = densities[:, part * width:(part + 1) * width]
        gamma_partial = gamma_over_aux(screened, dens_part)
        right_side = reduce_scatter_columns(gamma_partial, "pair")
        coefficients = solve(right_side, transfer, diag_inverse, sub_factor)
        coeff_full = all_gather_columns(coefficients, "pair")
        partial = contract_first(screened, coeff_full)
        results.append(lax.psum_scatter(partial, "aux", scatter_dimension=0, tiled=True))
    return jnp.concatenate(results, axis=1)


def solution(mesh):
    return jax.shard_map(
        per_device,
        mesh=mesh,
        in_specs=(
            P("aux", "pair"),
            P(("pair", "aux"), None),
            P("aux", "pair"),
            P("aux", None),
            P("aux", None),
        ),
        out_specs=P(("pair", "aux"), None),
        check_vma=False,
    )
```

```python
import jax
import jax.numpy as jnp
from jax import lax
from jax.sharding import PartitionSpec as P


def from_behind(array, axis, by):
    count = lax.axis_size(axis)
    pairs = [(i, i + by) for i in range(count) if 0 <= i + by < count]
    return lax.ppermute(array, axis, pairs)


def swap(array, axis, bit):
    count = lax.axis_size(axis)
    return lax.ppermute(array, axis, [(i, i ^ bit) for i in range(count)])


def screen_block(block, screen_mask):
    aux_blocks, pair_blocks = screen_mask.shape
    aux_size = block.shape[0] // aux_blocks
    pair_size = block.shape[1] // pair_blocks
    expanded = jnp.repeat(jnp.repeat(screen_mask.astype(jnp.float32), aux_size, 0), pair_size, 1)
    return block * expanded


def product(left, right):
    return jnp.dot(left, right, precision=lax.Precision.HIGH, preferred_element_type=jnp.float32)


def contract_first(left, right):
    return lax.dot_general(
        left,
        right,
        (((0,), (0,)), ((), ())),
        precision=lax.Precision.HIGH,
        preferred_element_type=jnp.float32,
    )


def reduce_scatter_columns(partial, axis):
    index = lax.axis_index(axis)
    count = lax.axis_size(axis)
    current = partial
    bit = 1
    while bit < count:
        width = current.shape[1] // 2
        low, high = current[:, :width], current[:, width:]
        upper = (index // bit) % 2 == 1
        send = jnp.where(upper, low, high)
        keep = jnp.where(upper, high, low)
        current = keep + swap(send, axis, bit)
        bit *= 2
    return current


def all_gather_columns(share, axis):
    index = lax.axis_index(axis)
    count = lax.axis_size(axis)
    current = share
    bit = count // 2
    while bit >= 1:
        other = swap(current, axis, bit)
        upper = (index // bit) % 2 == 1
        current = jnp.where(
            upper,
            jnp.concatenate([other, current], axis=1),
            jnp.concatenate([current, other], axis=1),
        )
        bit //= 2
    return current


def gamma_over_aux(screened, densities):
    count = lax.axis_size("aux")
    index = lax.axis_index("aux")
    rows = densities.shape[0]

    def columns(block):
        start = jnp.clip(block, 0, count - 1) * rows
        return lax.dynamic_slice_in_dim(screened, start, rows, axis=1)

    gamma = product(columns(index), densities)
    from_left, from_right = densities, densities
    for step in range(count - 1):
        from_left = from_behind(from_left, "aux", 1)
        from_right = from_behind(from_right, "aux", -1)
        gamma = gamma + product(columns(index - 1 - step), from_left)
        gamma = gamma + product(columns(index + 1 + step), from_right)
    return gamma


def reduce_over_aux(partial):
    count = lax.axis_size("aux")
    index = lax.axis_index("aux")
    rows = partial.shape[0] // count

    def block(owner):
        start = jnp.clip(owner, 0, count - 1) * rows
        return lax.dynamic_slice_in_dim(partial, start, rows, axis=0)

    to_right = jnp.zeros((rows, partial.shape[1]), partial.dtype)
    to_left = jnp.zeros((rows, partial.shape[1]), partial.dtype)
    for step in range(count - 1):
        to_right = from_behind(to_right + block(index + count - 1 - step), "aux", 1)
        to_left = from_behind(to_left + block(index - (count - 1) + step), "aux", -1)
    return to_right + to_left + block(index)


def gathered_position(axis):
    index = lax.axis_index(axis)
    count = lax.axis_size(axis)
    position = 0
    bit, mirror = 1, count // 2
    while bit < count:
        position = position + ((index // bit) % 2) * mirror
        bit, mirror = bit * 2, mirror // 2
    return position


def neighbour_maps(transfer):
    count = lax.axis_size("pair")
    width = transfer.shape[1] // count
    start = gathered_position("pair") * width
    mine = lax.dynamic_slice_in_dim(transfer, start, width, axis=1)
    pieces = jnp.concatenate(
        [from_behind(mine, "aux", 1), from_behind(mine, "aux", -1)], axis=1
    )
    full = all_gather_columns(pieces, "pair").reshape(transfer.shape[0], count, 2, width)
    rows = transfer.shape[0]
    return full[:, :, 0, :].reshape(rows, -1), full[:, :, 1, :].reshape(rows, -1)


def solve(right_side, transfer, two_step, next_map, diag_inverse):
    chain_length = lax.axis_size("aux")
    driving = product(diag_inverse, right_side)
    paired = driving + product(transfer, from_behind(driving, "aux", 1))
    solved = paired
    for _ in range(chain_length // 2 - 1):
        solved = paired + product(two_step, from_behind(solved, "aux", 2))
    solved_next = from_behind(driving, "aux", -1) + product(next_map, solved)
    back_map = next_map.T
    source = -product(back_map, solved_next)
    arriving = source
    for _ in range(chain_length - 2):
        arriving = source + product(back_map, from_behind(arriving, "aux", -1))
    return product(diag_inverse.T, solved - arriving)


SLICES = 2


def per_device(three_center, densities, screen_mask, diag_inverse, sub_factor):
    screened = screen_block(three_center, screen_mask)
    transfer = -product(diag_inverse, sub_factor)
    previous_map, next_map = neighbour_maps(transfer)
    two_step = product(transfer, previous_map)
    width = densities.shape[1] // SLICES
    results = []
    for part in range(SLICES):
        dens_part = densities[:, part * width:(part + 1) * width]
        gamma_partial = gamma_over_aux(screened, dens_part)
        right_side = reduce_scatter_columns(gamma_partial, "pair")
        coefficients = solve(right_side, transfer, two_step, next_map, diag_inverse)
        coeff_full = all_gather_columns(coefficients, "pair")
        partial = contract_first(screened, coeff_full)
        results.append(reduce_over_aux(partial))
    return jnp.concatenate(results, axis=1)


def solution(mesh):
    return jax.shard_map(
        per_device,
        mesh=mesh,
        in_specs=(
            P("aux", "pair"),
            P(("pair", "aux"), None),
            P("aux", "pair"),
            P("aux", None),
            P("aux", None),
        ),
        out_specs=P(("pair", "aux"), None),
        check_vma=False,
    )
```

```python
import functools

import jax
import jax.numpy as jnp
from jax import lax
from jax.experimental import pallas as pl
from jax.experimental.pallas import tpu as pltpu
from jax.sharding import PartitionSpec as P


def split3(x):
    high = x.astype(jnp.bfloat16)
    low = (x - high.astype(jnp.float32)).astype(jnp.bfloat16)
    return high, low


def dot3(a, b, dims):
    ah, al = split3(a)
    bh, bl = split3(b)
    f = functools.partial(lax.dot_general, dimension_numbers=(dims, ((), ())), preferred_element_type=jnp.float32)
    return f(ah, bh) + (f(ah, bl) + f(al, bh))


def expanded_mask(mask, rows, start_col, cols, row_size, col_size):
    mask_rows, mask_cols = mask.shape
    pick_rows = (lax.broadcasted_iota(jnp.int32, (rows, mask_rows), 0) // row_size
                 == lax.broadcasted_iota(jnp.int32, (rows, mask_rows), 1))
    pick_cols = (lax.broadcasted_iota(jnp.int32, (mask_cols, cols), 0)
                 == (lax.broadcasted_iota(jnp.int32, (mask_cols, cols), 1) + start_col) // col_size)
    by_rows = jnp.dot(pick_rows.astype(jnp.bfloat16), mask.astype(jnp.bfloat16), preferred_element_type=jnp.float32)
    return jnp.dot(by_rows.astype(jnp.bfloat16), pick_cols.astype(jnp.bfloat16), preferred_element_type=jnp.float32)


def gamma_kernel(block_ref, three_ref, mask_ref, dens_ref, acc_ref, out_ref, *, row_size, col_size, cut):
    rows, width = dens_ref.shape
    start = block_ref[0] * rows
    if cut:
        tile = three_ref[:, pl.ds(pl.multiple_of(start, 128), rows)]
    else:
        tile = three_ref[...]
    screened = tile * expanded_mask(mask_ref[...], tile.shape[0], start, rows, row_size, col_size)
    out_ref[...] = acc_ref[...] + dot3(screened, dens_ref[...], ((1,), (0,)))


def gamma_block(block, three_center, mask_f, dens, acc):
    rows_total, cols_total = three_center.shape
    row_size = rows_total // mask_f.shape[0]
    col_size = cols_total // mask_f.shape[1]
    rows = dens.shape[0]
    cut = rows % 128 == 0
    if not cut:
        three_center = lax.dynamic_slice_in_dim(three_center, block * rows, rows, axis=1)
    kernel = functools.partial(gamma_kernel, row_size=row_size, col_size=col_size, cut=cut)
    vmem = pl.BlockSpec(memory_space=pltpu.VMEM)
    return pl.pallas_call(
        kernel,
        out_shape=jax.ShapeDtypeStruct(acc.shape, jnp.float32),
        in_specs=[pl.BlockSpec(memory_space=pltpu.SMEM), vmem, vmem, vmem, vmem],
        out_specs=vmem,
        input_output_aliases={4: 0},
        cost_estimate=pl.CostEstimate(flops=6 * rows_total * rows * dens.shape[1], transcendentals=0,
                                      bytes_accessed=4 * (rows_total * rows + dens.size + 2 * acc.size)),
    )(jnp.reshape(block, (1,)).astype(jnp.int32), three_center, mask_f, dens, acc)


def response_kernel(three_ref, mask_ref, coef_ref, out_ref, *, row_size, col_size):
    rows, cols = three_ref.shape
    screened = three_ref[...] * expanded_mask(mask_ref[...], rows, 0, cols, row_size, col_size)
    out_ref[...] = dot3(screened, coef_ref[...], ((0,), (0,)))


def response(three_center, mask_f, coef):
    rows_total, cols_total = three_center.shape
    kernel = functools.partial(response_kernel, row_size=rows_total // mask_f.shape[0], col_size=cols_total // mask_f.shape[1])
    vmem = pl.BlockSpec(memory_space=pltpu.VMEM)
    return pl.pallas_call(
        kernel,
        out_shape=jax.ShapeDtypeStruct((cols_total, coef.shape[1]), jnp.float32),
        in_specs=[vmem, vmem, vmem],
        out_specs=vmem,
        cost_estimate=pl.CostEstimate(flops=6 * rows_total * cols_total * coef.shape[1], transcendentals=0,
                                      bytes_accessed=4 * (three_center.size + coef.size + cols_total * coef.shape[1])),
    )(three_center, mask_f, coef)


def from_behind(array, axis, by):
    count = lax.axis_size(axis)
    pairs = [(i, i + by) for i in range(count) if 0 <= i + by < count]
    return lax.ppermute(array, axis, pairs)


def swap(array, axis, bit):
    count = lax.axis_size(axis)
    return lax.ppermute(array, axis, [(i, i ^ bit) for i in range(count)])


def screen_block(block, screen_mask):
    aux_blocks, pair_blocks = screen_mask.shape
    aux_size = block.shape[0] // aux_blocks
    pair_size = block.shape[1] // pair_blocks
    expanded = jnp.repeat(jnp.repeat(screen_mask.astype(jnp.float32), aux_size, 0), pair_size, 1)
    return block * expanded


def product(left, right):
    return jnp.dot(left, right, precision=lax.Precision.HIGH, preferred_element_type=jnp.float32)


def contract_first(left, right):
    return lax.dot_general(
        left,
        right,
        (((0,), (0,)), ((), ())),
        precision=lax.Precision.HIGH,
        preferred_element_type=jnp.float32,
    )


def reduce_scatter_columns(partial, axis):
    index = lax.axis_index(axis)
    count = lax.axis_size(axis)
    current = partial
    bit = 1
    while bit < count:
        width = current.shape[1] // 2
        low, high = current[:, :width], current[:, width:]
        upper = (index // bit) % 2 == 1
        send = jnp.where(upper, low, high)
        keep = jnp.where(upper, high, low)
        current = keep + swap(send, axis, bit)
        bit *= 2
    return current


def all_gather_columns(share, axis):
    index = lax.axis_index(axis)
    count = lax.axis_size(axis)
    current = share
    bit = count // 2
    while bit >= 1:
        other = swap(current, axis, bit)
        upper = (index // bit) % 2 == 1
        current = jnp.where(
            upper,
            jnp.concatenate([other, current], axis=1),
            jnp.concatenate([current, other], axis=1),
        )
        bit //= 2
    return current


def gamma_over_aux(three_center, mask_f, densities):
    count = lax.axis_size("aux")
    index = lax.axis_index("aux")

    def clip(block):
        return jnp.clip(block, 0, count - 1)

    gamma = jnp.zeros((three_center.shape[0], densities.shape[1]), jnp.float32)
    gamma = gamma_block(index, three_center, mask_f, densities, gamma)
    from_left, from_right = densities, densities
    for step in range(count - 1):
        from_left = from_behind(from_left, "aux", 1)
        from_right = from_behind(from_right, "aux", -1)
        gamma = gamma_block(clip(index - 1 - step), three_center, mask_f, from_left, gamma)
        gamma = gamma_block(clip(index + 1 + step), three_center, mask_f, from_right, gamma)
    return gamma


def reduce_over_aux(partial):
    count = lax.axis_size("aux")
    index = lax.axis_index("aux")
    rows = partial.shape[0] // count

    def block(owner):
        start = jnp.clip(owner, 0, count - 1) * rows
        return lax.dynamic_slice_in_dim(partial, start, rows, axis=0)

    to_right = jnp.zeros((rows, partial.shape[1]), partial.dtype)
    to_left = jnp.zeros((rows, partial.shape[1]), partial.dtype)
    for step in range(count - 1):
        to_right = from_behind(to_right + block(index + count - 1 - step), "aux", 1)
        to_left = from_behind(to_left + block(index - (count - 1) + step), "aux", -1)
    return to_right + to_left + block(index)


def solve(right_side, transfer, diag_inverse, sub_factor):
    driving = product(diag_inverse, right_side)
    chain_length = lax.axis_size("aux")
    incoming = from_behind(driving, "aux", 1)
    for _ in range(chain_length - 2):
        incoming = from_behind(product(transfer, incoming) + driving, "aux", 1)
    solved = product(transfer, incoming) + driving
    source = product(sub_factor.T, product(diag_inverse.T, solved))
    back_map = transfer.T
    arriving = from_behind(source, "aux", -1)
    for _ in range(chain_length - 2):
        arriving = from_behind(product(back_map, arriving) + source, "aux", -1)
    return product(diag_inverse.T, solved - arriving)


SLICES = 2


def per_device(three_center, densities, screen_mask, diag_inverse, sub_factor):
    mask_f = screen_mask.astype(jnp.float32)
    transfer = -product(diag_inverse, sub_factor)
    width = densities.shape[1] // SLICES
    results = []
    for part in range(SLICES):
        dens_part = densities[:, part * width:(part + 1) * width]
        gamma_partial = gamma_over_aux(three_center, mask_f, dens_part)
        right_side = reduce_scatter_columns(gamma_partial, "pair")
        coefficients = solve(right_side, transfer, diag_inverse, sub_factor)
        coeff_full = all_gather_columns(coefficients, "pair")
        partial = response(three_center, mask_f, coeff_full)
        results.append(reduce_over_aux(partial))
    return jnp.concatenate(results, axis=1)


def solution(mesh):
    return jax.shard_map(
        per_device,
        mesh=mesh,
        in_specs=(
            P("aux", "pair"),
            P(("pair", "aux"), None),
            P("aux", "pair"),
            P("aux", None),
            P("aux", None),
        ),
        out_specs=P(("pair", "aux"), None),
        check_vma=False,
    )
```

```python
import functools

import jax
import jax.numpy as jnp
from jax import lax
from jax.experimental import pallas as pl
from jax.experimental.pallas import tpu as pltpu
from jax.sharding import PartitionSpec as P


def split3(x):
    high = x.astype(jnp.bfloat16)
    low = (x - high.astype(jnp.float32)).astype(jnp.bfloat16)
    return high, low


def dot3(a, b, dims):
    ah, al = split3(a)
    bh, bl = split3(b)
    f = functools.partial(lax.dot_general, dimension_numbers=(dims, ((), ())), preferred_element_type=jnp.float32)
    return f(ah, bh) + (f(ah, bl) + f(al, bh))


def expanded_mask(mask, rows, start_col, cols, row_size, col_size):
    mask_rows, mask_cols = mask.shape
    pick_rows = (lax.broadcasted_iota(jnp.int32, (rows, mask_rows), 0) // row_size
                 == lax.broadcasted_iota(jnp.int32, (rows, mask_rows), 1))
    pick_cols = (lax.broadcasted_iota(jnp.int32, (mask_cols, cols), 0)
                 == (lax.broadcasted_iota(jnp.int32, (mask_cols, cols), 1) + start_col) // col_size)
    by_rows = jnp.dot(pick_rows.astype(jnp.bfloat16), mask.astype(jnp.bfloat16), preferred_element_type=jnp.float32)
    return jnp.dot(by_rows.astype(jnp.bfloat16), pick_cols.astype(jnp.bfloat16), preferred_element_type=jnp.float32)


def gamma_kernel(block_ref, three_ref, mask_ref, dens_ref, acc_ref, out_ref, *, row_size, col_size):
    rows, width = dens_ref.shape
    start = block_ref[0] * rows
    tile = three_ref[...]
    screened = tile * expanded_mask(mask_ref[...], tile.shape[0], start, rows, row_size, col_size)
    out_ref[...] = acc_ref[...] + dot3(screened, dens_ref[...], ((1,), (0,)))


def gamma_block(block, three_center, mask_f, dens, acc):
    rows_total, cols_total = three_center.shape
    row_size = rows_total // mask_f.shape[0]
    col_size = cols_total // mask_f.shape[1]
    rows = dens.shape[0]
    block = jnp.reshape(block, (1,)).astype(jnp.int32)
    if rows % 128 == 0:
        tile_spec = pl.BlockSpec((rows_total, rows), lambda i, b: (0, b[0]))
    else:
        three_center = lax.dynamic_slice_in_dim(three_center, block[0] * rows, rows, axis=1)
        tile_spec = pl.BlockSpec((rows_total, rows), lambda i, b: (0, 0))
    kernel = functools.partial(gamma_kernel, row_size=row_size, col_size=col_size)
    whole = lambda i, b: (0, 0)
    return pl.pallas_call(
        kernel,
        out_shape=jax.ShapeDtypeStruct(acc.shape, jnp.float32),
        grid_spec=pltpu.PrefetchScalarGridSpec(
            num_scalar_prefetch=1,
            grid=(1,),
            in_specs=[
                tile_spec,
                pl.BlockSpec(mask_f.shape, whole),
                pl.BlockSpec(dens.shape, whole),
                pl.BlockSpec(acc.shape, whole),
            ],
            out_specs=pl.BlockSpec(acc.shape, whole),
        ),
        input_output_aliases={4: 0},
        cost_estimate=pl.CostEstimate(flops=6 * rows_total * rows * dens.shape[1], transcendentals=0,
                                      bytes_accessed=4 * (rows_total * rows + dens.size + 2 * acc.size)),
    )(block, three_center, mask_f, dens, acc)


def response_kernel(three_ref, mask_ref, coef_ref, out_ref, *, row_size, col_size):
    rows, cols = three_ref.shape
    start = pl.program_id(0) * cols
    screened = three_ref[...] * expanded_mask(mask_ref[...], rows, start, cols, row_size, col_size)
    out_ref[...] = dot3(screened, coef_ref[...], ((0,), (0,)))


def response(three_center, mask_f, coef):
    rows_total, cols_total = three_center.shape
    tile = 256 if cols_total % 256 == 0 else cols_total
    kernel = functools.partial(response_kernel, row_size=rows_total // mask_f.shape[0], col_size=cols_total // mask_f.shape[1])
    return pl.pallas_call(
        kernel,
        out_shape=jax.ShapeDtypeStruct((cols_total, coef.shape[1]), jnp.float32),
        grid=(cols_total // tile,),
        in_specs=[
            pl.BlockSpec((rows_total, tile), lambda j: (0, j)),
            pl.BlockSpec(mask_f.shape, lambda j: (0, 0)),
            pl.BlockSpec(coef.shape, lambda j: (0, 0)),
        ],
        out_specs=pl.BlockSpec((tile, coef.shape[1]), lambda j: (j, 0)),
        cost_estimate=pl.CostEstimate(flops=6 * rows_total * cols_total * coef.shape[1], transcendentals=0,
                                      bytes_accessed=4 * (three_center.size + coef.size + cols_total * coef.shape[1])),
    )(three_center, mask_f, coef)


def from_behind(array, axis, by):
    count = lax.axis_size(axis)
    pairs = [(i, i + by) for i in range(count) if 0 <= i + by < count]
    return lax.ppermute(array, axis, pairs)


def swap(array, axis, bit):
    count = lax.axis_size(axis)
    return lax.ppermute(array, axis, [(i, i ^ bit) for i in range(count)])


def screen_block(block, screen_mask):
    aux_blocks, pair_blocks = screen_mask.shape
    aux_size = block.shape[0] // aux_blocks
    pair_size = block.shape[1] // pair_blocks
    expanded = jnp.repeat(jnp.repeat(screen_mask.astype(jnp.float32), aux_size, 0), pair_size, 1)
    return block * expanded


def product(left, right):
    return jnp.dot(left, right, precision=lax.Precision.HIGH, preferred_element_type=jnp.float32)


def contract_first(left, right):
    return lax.dot_general(
        left,
        right,
        (((0,), (0,)), ((), ())),
        precision=lax.Precision.HIGH,
        preferred_element_type=jnp.float32,
    )


def reduce_scatter_columns(partial, axis):
    index = lax.axis_index(axis)
    count = lax.axis_size(axis)
    current = partial
    bit = 1
    while bit < count:
        width = current.shape[1] // 2
        low, high = current[:, :width], current[:, width:]
        upper = (index // bit) % 2 == 1
        send = jnp.where(upper, low, high)
        keep = jnp.where(upper, high, low)
        current = keep + swap(send, axis, bit)
        bit *= 2
    return current


def all_gather_columns(share, axis):
    index = lax.axis_index(axis)
    count = lax.axis_size(axis)
    current = share
    bit = count // 2
    while bit >= 1:
        other = swap(current, axis, bit)
        upper = (index // bit) % 2 == 1
        current = jnp.where(
            upper,
            jnp.concatenate([other, current], axis=1),
            jnp.concatenate([current, other], axis=1),
        )
        bit //= 2
    return current


def gamma_over_aux(three_center, mask_f, densities):
    count = lax.axis_size("aux")
    index = lax.axis_index("aux")

    def clip(block):
        return jnp.clip(block, 0, count - 1)

    gamma = jnp.zeros((three_center.shape[0], densities.shape[1]), jnp.float32)
    gamma = gamma_block(index, three_center, mask_f, densities, gamma)
    from_left, from_right = densities, densities
    for step in range(count - 1):
        from_left = from_behind(from_left, "aux", 1)
        from_right = from_behind(from_right, "aux", -1)
        gamma = gamma_block(clip(index - 1 - step), three_center, mask_f, from_left, gamma)
        gamma = gamma_block(clip(index + 1 + step), three_center, mask_f, from_right, gamma)
    return gamma


def reduce_over_aux(partial):
    count = lax.axis_size("aux")
    index = lax.axis_index("aux")
    rows = partial.shape[0] // count

    def block(owner):
        start = jnp.clip(owner, 0, count - 1) * rows
        return lax.dynamic_slice_in_dim(partial, start, rows, axis=0)

    to_right = jnp.zeros((rows, partial.shape[1]), partial.dtype)
    to_left = jnp.zeros((rows, partial.shape[1]), partial.dtype)
    for step in range(count - 1):
        to_right = from_behind(to_right + block(index + count - 1 - step), "aux", 1)
        to_left = from_behind(to_left + block(index - (count - 1) + step), "aux", -1)
    return to_right + to_left + block(index)


def solve(right_side, transfer, diag_inverse, sub_factor):
    driving = product(diag_inverse, right_side)
    chain_length = lax.axis_size("aux")
    incoming = from_behind(driving, "aux", 1)
    for _ in range(chain_length - 2):
        incoming = from_behind(product(transfer, incoming) + driving, "aux", 1)
    solved = product(transfer, incoming) + driving
    source = product(sub_factor.T, product(diag_inverse.T, solved))
    back_map = transfer.T
    arriving = from_behind(source, "aux", -1)
    for _ in range(chain_length - 2):
        arriving = from_behind(product(back_map, arriving) + source, "aux", -1)
    return product(diag_inverse.T, solved - arriving)


SLICES = 2


def per_device(three_center, densities, screen_mask, diag_inverse, sub_factor):
    mask_f = screen_mask.astype(jnp.float32)
    transfer = -product(diag_inverse, sub_factor)
    width = densities.shape[1] // SLICES
    results = []
    for part in range(SLICES):
        dens_part = densities[:, part * width:(part + 1) * width]
        gamma_partial = gamma_over_aux(three_center, mask_f, dens_part)
        right_side = reduce_scatter_columns(gamma_partial, "pair")
        coefficients = solve(right_side, transfer, diag_inverse, sub_factor)
        coeff_full = all_gather_columns(coefficients, "pair")
        partial = response(three_center, mask_f, coeff_full)
        results.append(reduce_over_aux(partial))
    return jnp.concatenate(results, axis=1)


def solution(mesh):
    return jax.shard_map(
        per_device,
        mesh=mesh,
        in_specs=(
            P("aux", "pair"),
            P(("pair", "aux"), None),
            P("aux", "pair"),
            P("aux", None),
            P("aux", None),
        ),
        out_specs=P(("pair", "aux"), None),
        check_vma=False,
    )
```

```python
import jax
import jax.numpy as jnp
from jax import lax
from jax.sharding import PartitionSpec as P


def from_behind(array, axis, by):
    count = lax.axis_size(axis)
    pairs = [(i, i + by) for i in range(count) if 0 <= i + by < count]
    return lax.ppermute(array, axis, pairs)


def swap(array, axis, bit):
    count = lax.axis_size(axis)
    return lax.ppermute(array, axis, [(i, i ^ bit) for i in range(count)])


def screen_block(block, screen_mask):
    aux_blocks, pair_blocks = screen_mask.shape
    aux_size = block.shape[0] // aux_blocks
    pair_size = block.shape[1] // pair_blocks
    expanded = jnp.repeat(jnp.repeat(screen_mask.astype(jnp.float32), aux_size, 0), pair_size, 1)
    return block * expanded


def product(left, right):
    return jnp.dot(left, right, precision=lax.Precision.HIGH, preferred_element_type=jnp.float32)


def contract_first(left, right):
    return lax.dot_general(
        left,
        right,
        (((0,), (0,)), ((), ())),
        precision=lax.Precision.HIGH,
        preferred_element_type=jnp.float32,
    )


def reduce_scatter_columns(partial, axis):
    index = lax.axis_index(axis)
    count = lax.axis_size(axis)
    current = partial
    bit = 1
    while bit < count:
        width = current.shape[1] // 2
        low, high = current[:, :width], current[:, width:]
        upper = (index // bit) % 2 == 1
        send = jnp.where(upper, low, high)
        keep = jnp.where(upper, high, low)
        current = keep + swap(send, axis, bit)
        bit *= 2
    return current


def all_gather_columns(share, axis):
    index = lax.axis_index(axis)
    count = lax.axis_size(axis)
    current = share
    bit = count // 2
    while bit >= 1:
        other = swap(current, axis, bit)
        upper = (index // bit) % 2 == 1
        current = jnp.where(
            upper,
            jnp.concatenate([other, current], axis=1),
            jnp.concatenate([current, other], axis=1),
        )
        bit //= 2
    return current


def gamma_over_aux(screened, densities):
    count = lax.axis_size("aux")
    index = lax.axis_index("aux")
    rows = densities.shape[0]

    def columns(block):
        start = jnp.clip(block, 0, count - 1) * rows
        return lax.dynamic_slice_in_dim(screened, start, rows, axis=1)

    gamma = product(columns(index), densities)
    from_left, from_right = densities, densities
    for step in range(count - 1):
        from_left = from_behind(from_left, "aux", 1)
        from_right = from_behind(from_right, "aux", -1)
        gamma = gamma + product(columns(index - 1 - step), from_left)
        gamma = gamma + product(columns(index + 1 + step), from_right)
    return gamma


def reduce_over_aux(partial):
    count = lax.axis_size("aux")
    index = lax.axis_index("aux")
    rows = partial.shape[0] // count

    def block(owner):
        start = jnp.clip(owner, 0, count - 1) * rows
        return lax.dynamic_slice_in_dim(partial, start, rows, axis=0)

    to_right = jnp.zeros((rows, partial.shape[1]), partial.dtype)
    to_left = jnp.zeros((rows, partial.shape[1]), partial.dtype)
    for step in range(count - 1):
        to_right = from_behind(to_right + block(index + count - 1 - step), "aux", 1)
        to_left = from_behind(to_left + block(index - (count - 1) + step), "aux", -1)
    return to_right + to_left + block(index)


def solve(right_side, transfer, diag_inverse, sub_factor):
    driving = product(diag_inverse, right_side)
    chain_length = lax.axis_size("aux")
    incoming = from_behind(driving, "aux", 1)
    for _ in range(chain_length - 2):
        incoming = from_behind(product(transfer, incoming) + driving, "aux", 1)
    solved = product(transfer, incoming) + driving
    source = product(sub_factor.T, product(diag_inverse.T, solved))
    back_map = transfer.T
    arriving = from_behind(source, "aux", -1)
    for _ in range(chain_length - 2):
        arriving = from_behind(product(back_map, arriving) + source, "aux", -1)
    return product(diag_inverse.T, solved - arriving)


SLICES = 1


def per_device(three_center, densities, screen_mask, diag_inverse, sub_factor):
    screened = screen_block(three_center, screen_mask)
    transfer = -product(diag_inverse, sub_factor)
    width = densities.shape[1] // SLICES
    results = []
    for part in range(SLICES):
        dens_part = densities[:, part * width:(part + 1) * width]
        gamma_partial = gamma_over_aux(screened, dens_part)
        right_side = reduce_scatter_columns(gamma_partial, "pair")
        coefficients = solve(right_side, transfer, diag_inverse, sub_factor)
        coeff_full = all_gather_columns(coefficients, "pair")
        partial = contract_first(screened, coeff_full)
        results.append(reduce_over_aux(partial))
    return jnp.concatenate(results, axis=1)


def solution(mesh):
    return jax.shard_map(
        per_device,
        mesh=mesh,
        in_specs=(
            P("aux", "pair"),
            P(("pair", "aux"), None),
            P("aux", "pair"),
            P("aux", None),
            P("aux", None),
        ),
        out_specs=P(("pair", "aux"), None),
        check_vma=False,
    )
```

```python
import jax
import jax.numpy as jnp
from jax import lax
from jax.sharding import PartitionSpec as P


def from_behind(array, axis, by):
    count = lax.axis_size(axis)
    pairs = [(i, i + by) for i in range(count) if 0 <= i + by < count]
    return lax.ppermute(array, axis, pairs)


def swap(array, axis, bit):
    count = lax.axis_size(axis)
    return lax.ppermute(array, axis, [(i, i ^ bit) for i in range(count)])


def screen_block(block, screen_mask):
    aux_blocks, pair_blocks = screen_mask.shape
    aux_size = block.shape[0] // aux_blocks
    pair_size = block.shape[1] // pair_blocks
    expanded = jnp.repeat(jnp.repeat(screen_mask.astype(jnp.float32), aux_size, 0), pair_size, 1)
    return block * expanded


def product(left, right):
    return jnp.dot(left, right, precision=lax.Precision.HIGH, preferred_element_type=jnp.float32)


def contract_first(left, right):
    return lax.dot_general(
        left,
        right,
        (((0,), (0,)), ((), ())),
        precision=lax.Precision.HIGH,
        preferred_element_type=jnp.float32,
    )


def reduce_scatter_columns(partial, axis):
    index = lax.axis_index(axis)
    count = lax.axis_size(axis)
    current = partial
    bit = 1
    while bit < count:
        width = current.shape[1] // 2
        low, high = current[:, :width], current[:, width:]
        upper = (index // bit) % 2 == 1
        send = jnp.where(upper, low, high)
        keep = jnp.where(upper, high, low)
        current = keep + swap(send, axis, bit)
        bit *= 2
    return current


def all_gather_columns(share, axis):
    index = lax.axis_index(axis)
    count = lax.axis_size(axis)
    current = share
    bit = count // 2
    while bit >= 1:
        other = swap(current, axis, bit)
        upper = (index // bit) % 2 == 1
        current = jnp.where(
            upper,
            jnp.concatenate([other, current], axis=1),
            jnp.concatenate([current, other], axis=1),
        )
        bit //= 2
    return current


def gamma_over_aux(screened, densities):
    count = lax.axis_size("aux")
    index = lax.axis_index("aux")
    rows = densities.shape[0]

    def columns(block):
        start = jnp.clip(block, 0, count - 1) * rows
        return lax.dynamic_slice_in_dim(screened, start, rows, axis=1)

    gamma = product(columns(index), densities)
    from_left, from_right = densities, densities
    for step in range(count - 1):
        from_left = from_behind(from_left, "aux", 1)
        from_right = from_behind(from_right, "aux", -1)
        gamma = gamma + product(columns(index - 1 - step), from_left)
        gamma = gamma + product(columns(index + 1 + step), from_right)
    return gamma


def reduce_over_aux(partial):
    count = lax.axis_size("aux")
    index = lax.axis_index("aux")
    rows = partial.shape[0] // count

    def block(owner):
        start = jnp.clip(owner, 0, count - 1) * rows
        return lax.dynamic_slice_in_dim(partial, start, rows, axis=0)

    to_right = jnp.zeros((rows, partial.shape[1]), partial.dtype)
    to_left = jnp.zeros((rows, partial.shape[1]), partial.dtype)
    for step in range(count - 1):
        to_right = from_behind(to_right + block(index + count - 1 - step), "aux", 1)
        to_left = from_behind(to_left + block(index - (count - 1) + step), "aux", -1)
    return to_right + to_left + block(index)


def solve(right_side, transfer, diag_inverse, sub_factor):
    driving = product(diag_inverse, right_side)
    chain_length = lax.axis_size("aux")
    incoming = from_behind(driving, "aux", 1)
    for _ in range(chain_length - 2):
        incoming = from_behind(product(transfer, incoming) + driving, "aux", 1)
    solved = product(transfer, incoming) + driving
    source = product(sub_factor.T, product(diag_inverse.T, solved))
    back_map = transfer.T
    arriving = from_behind(source, "aux", -1)
    for _ in range(chain_length - 2):
        arriving = from_behind(product(back_map, arriving) + source, "aux", -1)
    return product(diag_inverse.T, solved - arriving)


SLICES = 2


def per_device(three_center, densities, screen_mask, diag_inverse, sub_factor):
    screened = screen_block(three_center, screen_mask)
    transfer = -product(diag_inverse, sub_factor)
    width = densities.shape[1] // SLICES
    results = []
    gate = None
    for part in range(SLICES):
        dens_part = densities[:, part * width:(part + 1) * width]
        if gate is not None:
            dens_part, _ = lax.optimization_barrier((dens_part, gate))
        gamma_partial = gamma_over_aux(screened, dens_part)
        right_side = reduce_scatter_columns(gamma_partial, "pair")
        gate = right_side
        coefficients = solve(right_side, transfer, diag_inverse, sub_factor)
        coeff_full = all_gather_columns(coefficients, "pair")
        partial = contract_first(screened, coeff_full)
        results.append(reduce_over_aux(partial))
    return jnp.concatenate(results, axis=1)


def solution(mesh):
    return jax.shard_map(
        per_device,
        mesh=mesh,
        in_specs=(
            P("aux", "pair"),
            P(("pair", "aux"), None),
            P("aux", "pair"),
            P("aux", None),
            P("aux", None),
        ),
        out_specs=P(("pair", "aux"), None),
        check_vma=False,
    )
```

```python
import jax
import jax.numpy as jnp
from jax import lax
from jax.sharding import PartitionSpec as P


def from_behind(array, axis, by):
    count = lax.axis_size(axis)
    pairs = [(i, i + by) for i in range(count) if 0 <= i + by < count]
    return lax.ppermute(array, axis, pairs)


def swap(array, axis, bit):
    count = lax.axis_size(axis)
    return lax.ppermute(array, axis, [(i, i ^ bit) for i in range(count)])


def screen_block(block, screen_mask):
    aux_blocks, pair_blocks = screen_mask.shape
    aux_size = block.shape[0] // aux_blocks
    pair_size = block.shape[1] // pair_blocks
    expanded = jnp.repeat(jnp.repeat(screen_mask.astype(jnp.float32), aux_size, 0), pair_size, 1)
    return block * expanded


def product(left, right):
    return jnp.dot(left, right, precision=lax.Precision.HIGH, preferred_element_type=jnp.float32)


def contract_first(left, right):
    return lax.dot_general(
        left,
        right,
        (((0,), (0,)), ((), ())),
        precision=lax.Precision.HIGH,
        preferred_element_type=jnp.float32,
    )


def reduce_scatter_columns(partial, axis):
    index = lax.axis_index(axis)
    count = lax.axis_size(axis)
    current = partial
    bit = 1
    while bit < count:
        width = current.shape[1] // 2
        low, high = current[:, :width], current[:, width:]
        upper = (index // bit) % 2 == 1
        send = jnp.where(upper, low, high)
        keep = jnp.where(upper, high, low)
        current = keep + swap(send, axis, bit)
        bit *= 2
    return current


def all_gather_columns(share, axis):
    index = lax.axis_index(axis)
    count = lax.axis_size(axis)
    current = share
    bit = count // 2
    while bit >= 1:
        other = swap(current, axis, bit)
        upper = (index // bit) % 2 == 1
        current = jnp.where(
            upper,
            jnp.concatenate([other, current], axis=1),
            jnp.concatenate([current, other], axis=1),
        )
        bit //= 2
    return current


def gamma_over_aux(screened, densities):
    count = lax.axis_size("aux")
    index = lax.axis_index("aux")
    rows = densities.shape[0]

    def columns(block):
        start = jnp.clip(block, 0, count - 1) * rows
        return lax.dynamic_slice_in_dim(screened, start, rows, axis=1)

    gamma = product(columns(index), densities)
    from_left, from_right = densities, densities
    for step in range(count - 1):
        from_left = from_behind(from_left, "aux", 1)
        from_right = from_behind(from_right, "aux", -1)
        gamma = gamma + product(columns(index - 1 - step), from_left)
        gamma = gamma + product(columns(index + 1 + step), from_right)
    return gamma


def reduce_over_aux(partial):
    count = lax.axis_size("aux")
    index = lax.axis_index("aux")
    rows = partial.shape[0] // count

    def block(owner):
        start = jnp.clip(owner, 0, count - 1) * rows
        return lax.dynamic_slice_in_dim(partial, start, rows, axis=0)

    to_right = jnp.zeros((rows, partial.shape[1]), partial.dtype)
    to_left = jnp.zeros((rows, partial.shape[1]), partial.dtype)
    for step in range(count - 1):
        to_right = from_behind(to_right + block(index + count - 1 - step), "aux", 1)
        to_left = from_behind(to_left + block(index - (count - 1) + step), "aux", -1)
    return to_right + to_left + block(index)


def solve(right_side, transfer, diag_inverse, sub_factor):
    driving = product(diag_inverse, right_side)
    chain_length = lax.axis_size("aux")
    incoming = from_behind(driving, "aux", 1)
    for _ in range(chain_length - 2):
        incoming = from_behind(product(transfer, incoming) + driving, "aux", 1)
    solved = product(transfer, incoming) + driving
    source = product(sub_factor.T, product(diag_inverse.T, solved))
    back_map = transfer.T
    arriving = from_behind(source, "aux", -1)
    for _ in range(chain_length - 2):
        arriving = from_behind(product(back_map, arriving) + source, "aux", -1)
    return product(diag_inverse.T, solved - arriving)


SLICES = 2


def per_device(three_center, densities, screen_mask, diag_inverse, sub_factor):
    screened = screen_block(three_center, screen_mask)
    transfer = -product(diag_inverse, sub_factor)
    gamma_partial = gamma_over_aux(screened, densities)
    width = gamma_partial.shape[1] // SLICES
    results = []
    for part in range(SLICES):
        right_side = reduce_scatter_columns(gamma_partial[:, part * width:(part + 1) * width], "pair")
        coefficients = solve(right_side, transfer, diag_inverse, sub_factor)
        coeff_full = all_gather_columns(coefficients, "pair")
        partial = contract_first(screened, coeff_full)
        results.append(reduce_over_aux(partial))
    return jnp.concatenate(results, axis=1)


def solution(mesh):
    return jax.shard_map(
        per_device,
        mesh=mesh,
        in_specs=(
            P("aux", "pair"),
            P(("pair", "aux"), None),
            P("aux", "pair"),
            P("aux", None),
            P("aux", None),
        ),
        out_specs=P(("pair", "aux"), None),
        check_vma=False,
    )
```

```python
import jax
import jax.numpy as jnp
from jax import lax
from jax.sharding import PartitionSpec as P


def from_behind(array, axis, by):
    count = lax.axis_size(axis)
    pairs = [(i, i + by) for i in range(count) if 0 <= i + by < count]
    return lax.ppermute(array, axis, pairs)


def swap(array, axis, bit):
    count = lax.axis_size(axis)
    return lax.ppermute(array, axis, [(i, i ^ bit) for i in range(count)])


def screen_block(block, screen_mask):
    aux_blocks, pair_blocks = screen_mask.shape
    aux_size = block.shape[0] // aux_blocks
    pair_size = block.shape[1] // pair_blocks
    expanded = jnp.repeat(jnp.repeat(screen_mask.astype(jnp.float32), aux_size, 0), pair_size, 1)
    return block * expanded


def product(left, right):
    return jnp.dot(left, right, precision=lax.Precision.HIGH, preferred_element_type=jnp.float32)


def contract_first(left, right):
    return lax.dot_general(
        left,
        right,
        (((0,), (0,)), ((), ())),
        precision=lax.Precision.HIGH,
        preferred_element_type=jnp.float32,
    )


def reduce_scatter_columns(partial, axis):
    index = lax.axis_index(axis)
    count = lax.axis_size(axis)
    current = partial
    bit = 1
    while bit < count:
        width = current.shape[1] // 2
        low, high = current[:, :width], current[:, width:]
        upper = (index // bit) % 2 == 1
        send = jnp.where(upper, low, high)
        keep = jnp.where(upper, high, low)
        current = keep + swap(send, axis, bit)
        bit *= 2
    return current


def all_gather_columns(share, axis):
    index = lax.axis_index(axis)
    count = lax.axis_size(axis)
    current = share
    bit = count // 2
    while bit >= 1:
        other = swap(current, axis, bit)
        upper = (index // bit) % 2 == 1
        current = jnp.where(
            upper,
            jnp.concatenate([other, current], axis=1),
            jnp.concatenate([current, other], axis=1),
        )
        bit //= 2
    return current


def gamma_over_aux(screened, densities):
    count = lax.axis_size("aux")
    index = lax.axis_index("aux")
    rows = densities.shape[0]

    def columns(block):
        start = jnp.clip(block, 0, count - 1) * rows
        return lax.dynamic_slice_in_dim(screened, start, rows, axis=1)

    gamma = product(columns(index), densities)
    from_left, from_right = densities, densities
    for step in range(count - 1):
        from_left = from_behind(from_left, "aux", 1)
        from_right = from_behind(from_right, "aux", -1)
        gamma = gamma + product(columns(index - 1 - step), from_left)
        gamma = gamma + product(columns(index + 1 + step), from_right)
    return gamma


def reduce_over_aux(partial):
    count = lax.axis_size("aux")
    index = lax.axis_index("aux")
    rows = partial.shape[0] // count

    def block(owner):
        start = jnp.clip(owner, 0, count - 1) * rows
        return lax.dynamic_slice_in_dim(partial, start, rows, axis=0)

    to_right = jnp.zeros((rows, partial.shape[1]), partial.dtype)
    to_left = jnp.zeros((rows, partial.shape[1]), partial.dtype)
    for step in range(count - 1):
        to_right = from_behind(to_right + block(index + count - 1 - step), "aux", 1)
        to_left = from_behind(to_left + block(index - (count - 1) + step), "aux", -1)
    return to_right + to_left + block(index)


def solve(right_side, transfer, diag_inverse, sub_factor):
    driving = product(diag_inverse, right_side)
    chain_length = lax.axis_size("aux")
    incoming = from_behind(driving, "aux", 1)
    for _ in range(chain_length - 2):
        incoming = from_behind(product(transfer, incoming) + driving, "aux", 1)
    solved = product(transfer, incoming) + driving
    source = product(sub_factor.T, product(diag_inverse.T, solved))
    back_map = transfer.T
    arriving = from_behind(source, "aux", -1)
    for _ in range(chain_length - 2):
        arriving = from_behind(product(back_map, arriving) + source, "aux", -1)
    return product(diag_inverse.T, solved - arriving)


SLICES = 4


def per_device(three_center, densities, screen_mask, diag_inverse, sub_factor):
    screened = screen_block(three_center, screen_mask)
    transfer = -product(diag_inverse, sub_factor)
    gamma_partial = gamma_over_aux(screened, densities)
    width = gamma_partial.shape[1] // SLICES
    results = []
    for part in range(SLICES):
        right_side = reduce_scatter_columns(gamma_partial[:, part * width:(part + 1) * width], "pair")
        coefficients = solve(right_side, transfer, diag_inverse, sub_factor)
        coeff_full = all_gather_columns(coefficients, "pair")
        partial = contract_first(screened, coeff_full)
        results.append(reduce_over_aux(partial))
    return jnp.concatenate(results, axis=1)


def solution(mesh):
    return jax.shard_map(
        per_device,
        mesh=mesh,
        in_specs=(
            P("aux", "pair"),
            P(("pair", "aux"), None),
            P("aux", "pair"),
            P("aux", None),
            P("aux", None),
        ),
        out_specs=P(("pair", "aux"), None),
        check_vma=False,
    )
```

```python
import jax
import jax.numpy as jnp
from jax import lax
from jax.sharding import PartitionSpec as P


def from_behind(array, axis, by):
    count = lax.axis_size(axis)
    pairs = [(i, i + by) for i in range(count) if 0 <= i + by < count]
    return lax.ppermute(array, axis, pairs)


def swap(array, axis, bit):
    count = lax.axis_size(axis)
    return lax.ppermute(array, axis, [(i, i ^ bit) for i in range(count)])


def screen_block(block, screen_mask):
    aux_blocks, pair_blocks = screen_mask.shape
    aux_size = block.shape[0] // aux_blocks
    pair_size = block.shape[1] // pair_blocks
    expanded = jnp.repeat(jnp.repeat(screen_mask.astype(jnp.float32), aux_size, 0), pair_size, 1)
    return block * expanded


def product(left, right):
    return jnp.dot(left, right, precision=lax.Precision.HIGH, preferred_element_type=jnp.float32)


def contract_first(left, right):
    return lax.dot_general(
        left,
        right,
        (((0,), (0,)), ((), ())),
        precision=lax.Precision.HIGH,
        preferred_element_type=jnp.float32,
    )


def reduce_scatter_columns(partial, axis):
    index = lax.axis_index(axis)
    count = lax.axis_size(axis)
    current = partial
    bit = 1
    while bit < count:
        width = current.shape[1] // 2
        low, high = current[:, :width], current[:, width:]
        upper = (index // bit) % 2 == 1
        send = jnp.where(upper, low, high)
        keep = jnp.where(upper, high, low)
        current = keep + swap(send, axis, bit)
        bit *= 2
    return current


def all_gather_columns(share, axis):
    index = lax.axis_index(axis)
    count = lax.axis_size(axis)
    current = share
    bit = count // 2
    while bit >= 1:
        other = swap(current, axis, bit)
        upper = (index // bit) % 2 == 1
        current = jnp.where(
            upper,
            jnp.concatenate([other, current], axis=1),
            jnp.concatenate([current, other], axis=1),
        )
        bit //= 2
    return current


def gamma_over_aux(screened, densities):
    count = lax.axis_size("aux")
    index = lax.axis_index("aux")
    rows = densities.shape[0]

    def columns(block):
        start = jnp.clip(block, 0, count - 1) * rows
        return lax.dynamic_slice_in_dim(screened, start, rows, axis=1)

    gamma = product(columns(index), densities)
    from_left, from_right = densities, densities
    for step in range(count - 1):
        from_left = from_behind(from_left, "aux", 1)
        from_right = from_behind(from_right, "aux", -1)
        gamma = gamma + product(columns(index - 1 - step), from_left)
        gamma = gamma + product(columns(index + 1 + step), from_right)
    return gamma


def reduce_over_aux(partial):
    count = lax.axis_size("aux")
    index = lax.axis_index("aux")
    rows = partial.shape[0] // count

    def block(owner):
        start = jnp.clip(owner, 0, count - 1) * rows
        return lax.dynamic_slice_in_dim(partial, start, rows, axis=0)

    to_right = jnp.zeros((rows, partial.shape[1]), partial.dtype)
    to_left = jnp.zeros((rows, partial.shape[1]), partial.dtype)
    for step in range(count - 1):
        to_right = from_behind(to_right + block(index + count - 1 - step), "aux", 1)
        to_left = from_behind(to_left + block(index - (count - 1) + step), "aux", -1)
    return to_right + to_left + block(index)


def solve(right_side, transfer, diag_inverse, sub_factor):
    driving = product(diag_inverse, right_side)
    chain_length = lax.axis_size("aux")
    incoming = from_behind(driving, "aux", 1)
    for _ in range(chain_length - 2):
        incoming = from_behind(product(transfer, incoming) + driving, "aux", 1)
    solved = product(transfer, incoming) + driving
    source = product(sub_factor.T, product(diag_inverse.T, solved))
    back_map = transfer.T
    arriving = from_behind(source, "aux", -1)
    for _ in range(chain_length - 2):
        arriving = from_behind(product(back_map, arriving) + source, "aux", -1)
    return product(diag_inverse.T, solved - arriving)


SLICES = 2


def per_device(three_center, densities, screen_mask, diag_inverse, sub_factor):
    screened = screen_block(three_center, screen_mask)
    transfer = -product(diag_inverse, sub_factor)
    gamma_partial = gamma_over_aux(screened, densities)
    right_side = reduce_scatter_columns(gamma_partial, "pair")
    width = right_side.shape[1] // SLICES
    results = []
    for part in range(SLICES):
        coefficients = solve(right_side[:, part * width:(part + 1) * width], transfer, diag_inverse, sub_factor)
        coeff_full = all_gather_columns(coefficients, "pair")
        partial = contract_first(screened, coeff_full)
        results.append(reduce_over_aux(partial).reshape(partial.shape[0] // lax.axis_size("aux"), -1, width))
    joined = jnp.concatenate(results, axis=2)
    return joined.reshape(joined.shape[0], -1)


def solution(mesh):
    return jax.shard_map(
        per_device,
        mesh=mesh,
        in_specs=(
            P("aux", "pair"),
            P(("pair", "aux"), None),
            P("aux", "pair"),
            P("aux", None),
            P("aux", None),
        ),
        out_specs=P(("pair", "aux"), None),
        check_vma=False,
    )
```

```python
import jax
import jax.numpy as jnp
from jax import lax
from jax.sharding import PartitionSpec as P


def from_behind(array, axis, by):
    count = lax.axis_size(axis)
    pairs = [(i, i + by) for i in range(count) if 0 <= i + by < count]
    return lax.ppermute(array, axis, pairs)


def swap(array, axis, bit):
    count = lax.axis_size(axis)
    return lax.ppermute(array, axis, [(i, i ^ bit) for i in range(count)])


def screen_block(block, screen_mask):
    aux_blocks, pair_blocks = screen_mask.shape
    aux_size = block.shape[0] // aux_blocks
    pair_size = block.shape[1] // pair_blocks
    expanded = jnp.repeat(jnp.repeat(screen_mask.astype(jnp.float32), aux_size, 0), pair_size, 1)
    return block * expanded


def product(left, right):
    return jnp.dot(left, right, precision=lax.Precision.HIGH, preferred_element_type=jnp.float32)


def contract_first(left, right):
    return lax.dot_general(
        left,
        right,
        (((0,), (0,)), ((), ())),
        precision=lax.Precision.HIGH,
        preferred_element_type=jnp.float32,
    )


def reduce_scatter_columns(partial, axis):
    index = lax.axis_index(axis)
    count = lax.axis_size(axis)
    current = partial
    bit = 1
    while bit < count:
        width = current.shape[-1] // 2
        low, high = current[..., :width], current[..., width:]
        upper = (index // bit) % 2 == 1
        send = jnp.where(upper, low, high)
        keep = jnp.where(upper, high, low)
        current = keep + swap(send, axis, bit)
        bit *= 2
    return current


def all_gather_columns(share, axis):
    index = lax.axis_index(axis)
    count = lax.axis_size(axis)
    current = share
    bit = count // 2
    while bit >= 1:
        other = swap(current, axis, bit)
        upper = (index // bit) % 2 == 1
        current = jnp.where(
            upper,
            jnp.concatenate([other, current], axis=1),
            jnp.concatenate([current, other], axis=1),
        )
        bit //= 2
    return current


def gamma_over_aux(screened, densities):
    count = lax.axis_size("aux")
    index = lax.axis_index("aux")
    rows = densities.shape[0]

    def columns(block):
        start = jnp.clip(block, 0, count - 1) * rows
        return lax.dynamic_slice_in_dim(screened, start, rows, axis=1)

    gamma = product(columns(index), densities)
    helped = count >= 4
    steps = count - 2 if helped else count - 1
    from_left, from_right = densities, densities
    for step in range(steps):
        rightward = [(i, i + 1) for i in range(step, count - 1)]
        leftward = [(i + 1, i) for i in range(count - 1 - step)]
        from_left = lax.ppermute(from_left, "aux", rightward)
        from_right = lax.ppermute(from_right, "aux", leftward)
        gamma = gamma + product(columns(index - 1 - step), from_left)
        gamma = gamma + product(columns(index + 1 + step), from_right)
    if not helped:
        return gamma, jnp.zeros_like(gamma)
    end_pairs = [(0, 1), (count - 1, count - 2)]
    end_columns = lax.ppermute(columns(jnp.where(index == 0, count - 1, 0)), "aux", end_pairs)
    far = product(end_columns, jnp.where(index == 1, from_right, from_left))
    return gamma, far


def return_far(far_share):
    count = lax.axis_size("aux")
    if count < 4:
        return far_share
    return lax.ppermute(far_share, "aux", [(1, 0), (count - 2, count - 1)])


def reduce_over_aux(partial):
    count = lax.axis_size("aux")
    index = lax.axis_index("aux")
    rows = partial.shape[0] // count

    def block(owner):
        start = jnp.clip(owner, 0, count - 1) * rows
        return lax.dynamic_slice_in_dim(partial, start, rows, axis=0)

    to_right = jnp.zeros((rows, partial.shape[1]), partial.dtype)
    to_left = jnp.zeros((rows, partial.shape[1]), partial.dtype)
    for step in range(count - 1):
        to_right = from_behind(to_right + block(index + count - 1 - step), "aux", 1)
        to_left = from_behind(to_left + block(index - (count - 1) + step), "aux", -1)
    return to_right + to_left + block(index)


def solve(right_side, transfer, diag_inverse, sub_factor):
    driving = product(diag_inverse, right_side)
    chain_length = lax.axis_size("aux")
    incoming = from_behind(driving, "aux", 1)
    for _ in range(chain_length - 2):
        incoming = from_behind(product(transfer, incoming) + driving, "aux", 1)
    solved = product(transfer, incoming) + driving
    source = product(sub_factor.T, product(diag_inverse.T, solved))
    back_map = transfer.T
    arriving = from_behind(source, "aux", -1)
    for _ in range(chain_length - 2):
        arriving = from_behind(product(back_map, arriving) + source, "aux", -1)
    return product(diag_inverse.T, solved - arriving)


SLICES = 2


def per_device(three_center, densities, screen_mask, diag_inverse, sub_factor):
    screened = screen_block(three_center, screen_mask)
    transfer = -product(diag_inverse, sub_factor)
    gamma_partial, far = gamma_over_aux(screened, densities)
    width = gamma_partial.shape[1] // SLICES
    results = []
    for part in range(SLICES):
        columns = slice(part * width, (part + 1) * width)
        both = reduce_scatter_columns(jnp.stack([gamma_partial[:, columns], far[:, columns]]), "pair")
        right_side = both[0] + return_far(both[1])
        coefficients = solve(right_side, transfer, diag_inverse, sub_factor)
        coeff_full = all_gather_columns(coefficients, "pair")
        partial = contract_first(screened, coeff_full)
        results.append(reduce_over_aux(partial))
    return jnp.concatenate(results, axis=1)


def solution(mesh):
    return jax.shard_map(
        per_device,
        mesh=mesh,
        in_specs=(
            P("aux", "pair"),
            P(("pair", "aux"), None),
            P("aux", "pair"),
            P("aux", None),
            P("aux", None),
        ),
        out_specs=P(("pair", "aux"), None),
        check_vma=False,
    )
```

```python
import jax
import jax.numpy as jnp
from jax import lax
from jax.sharding import PartitionSpec as P


def from_behind(array, axis, by):
    count = lax.axis_size(axis)
    pairs = [(i, i + by) for i in range(count) if 0 <= i + by < count]
    return lax.ppermute(array, axis, pairs)


def swap(array, axis, bit):
    count = lax.axis_size(axis)
    return lax.ppermute(array, axis, [(i, i ^ bit) for i in range(count)])


def screen_block(block, screen_mask):
    aux_blocks, pair_blocks = screen_mask.shape
    aux_size = block.shape[0] // aux_blocks
    pair_size = block.shape[1] // pair_blocks
    expanded = jnp.repeat(jnp.repeat(screen_mask.astype(jnp.float32), aux_size, 0), pair_size, 1)
    return block * expanded


def product(left, right):
    return jnp.dot(left, right, precision=lax.Precision.HIGH, preferred_element_type=jnp.float32)


def contract_first(left, right):
    return lax.dot_general(
        left,
        right,
        (((0,), (0,)), ((), ())),
        precision=lax.Precision.HIGH,
        preferred_element_type=jnp.float32,
    )


def reduce_scatter_columns(partial, axis):
    index = lax.axis_index(axis)
    count = lax.axis_size(axis)
    current = partial
    bit = 1
    while bit < count:
        width = current.shape[1] // 2
        low, high = current[:, :width], current[:, width:]
        upper = (index // bit) % 2 == 1
        send = jnp.where(upper, low, high)
        keep = jnp.where(upper, high, low)
        current = keep + swap(send, axis, bit)
        bit *= 2
    return current


def all_gather_columns(share, axis):
    index = lax.axis_index(axis)
    count = lax.axis_size(axis)
    current = share
    bit = count // 2
    while bit >= 1:
        other = swap(current, axis, bit)
        upper = (index // bit) % 2 == 1
        current = jnp.where(
            upper,
            jnp.concatenate([other, current], axis=1),
            jnp.concatenate([current, other], axis=1),
        )
        bit //= 2
    return current


def gamma_over_aux(screened, densities):
    count = lax.axis_size("aux")
    index = lax.axis_index("aux")
    rows = densities.shape[0]

    def columns(block):
        start = jnp.clip(block, 0, count - 1) * rows
        return lax.dynamic_slice_in_dim(screened, start, rows, axis=1)

    gamma = product(columns(index), densities)
    from_left, from_right = densities, densities
    for step in range(count - 1):
        from_left = from_behind(from_left, "aux", 1)
        from_right = from_behind(from_right, "aux", -1)
        gamma = gamma + product(columns(index - 1 - step), from_left)
        gamma = gamma + product(columns(index + 1 + step), from_right)
    return gamma


def reduce_over_aux(partial):
    count = lax.axis_size("aux")
    index = lax.axis_index("aux")
    rows = partial.shape[0] // count

    def block(owner):
        start = jnp.clip(owner, 0, count - 1) * rows
        return lax.dynamic_slice_in_dim(partial, start, rows, axis=0)

    to_right = jnp.zeros((rows, partial.shape[1]), partial.dtype)
    to_left = jnp.zeros((rows, partial.shape[1]), partial.dtype)
    for step in range(count - 1):
        to_right = from_behind(to_right + block(index + count - 1 - step), "aux", 1)
        to_left = from_behind(to_left + block(index - (count - 1) + step), "aux", -1)
    return to_right + to_left + block(index)


def gathered_position(axis):
    index = lax.axis_index(axis)
    count = lax.axis_size(axis)
    position = 0
    bit, mirror = 1, count // 2
    while bit < count:
        position = position + ((index // bit) % 2) * mirror
        bit, mirror = bit * 2, mirror // 2
    return position


def neighbour_maps(transfer):
    count = lax.axis_size("pair")
    width = transfer.shape[1] // count
    start = gathered_position("pair") * width
    mine = lax.dynamic_slice_in_dim(transfer, start, width, axis=1)
    pieces = jnp.concatenate(
        [from_behind(mine, "aux", 1), from_behind(mine, "aux", -1)], axis=1
    )
    full = all_gather_columns(pieces, "pair").reshape(transfer.shape[0], count, 2, width)
    rows = transfer.shape[0]
    return full[:, :, 0, :].reshape(rows, -1), full[:, :, 1, :].reshape(rows, -1)


def solve(right_side, transfer, two_step, next_map, diag_inverse):
    chain_length = lax.axis_size("aux")
    driving = product(diag_inverse, right_side)
    paired = driving + product(transfer, from_behind(driving, "aux", 1))
    solved = paired
    for _ in range(chain_length // 2 - 1):
        solved = paired + product(two_step, from_behind(solved, "aux", 2))
    solved_next = from_behind(driving, "aux", -1) + product(next_map, solved)
    back_map = next_map.T
    source = -product(back_map, solved_next)
    arriving = source
    for _ in range(chain_length - 2):
        arriving = source + product(back_map, from_behind(arriving, "aux", -1))
    return product(diag_inverse.T, solved - arriving)


SLICES = 2


def per_device(three_center, densities, screen_mask, diag_inverse, sub_factor):
    screened = screen_block(three_center, screen_mask)
    transfer = -product(diag_inverse, sub_factor)
    previous_map, next_map = neighbour_maps(transfer)
    two_step = product(transfer, previous_map)
    gamma_partial = gamma_over_aux(screened, densities)
    width = gamma_partial.shape[1] // SLICES
    results = []
    for part in range(SLICES):
        right_side = reduce_scatter_columns(gamma_partial[:, part * width:(part + 1) * width], "pair")
        coefficients = solve(right_side, transfer, two_step, next_map, diag_inverse)
        coeff_full = all_gather_columns(coefficients, "pair")
        partial = contract_first(screened, coeff_full)
        results.append(reduce_over_aux(partial))
    return jnp.concatenate(results, axis=1)


def solution(mesh):
    return jax.shard_map(
        per_device,
        mesh=mesh,
        in_specs=(
            P("aux", "pair"),
            P(("pair", "aux"), None),
            P("aux", "pair"),
            P("aux", None),
            P("aux", None),
        ),
        out_specs=P(("pair", "aux"), None),
        check_vma=False,
    )
```

```python
import jax
import jax.numpy as jnp
from jax import lax
from jax.sharding import PartitionSpec as P


def from_behind(array, axis, by):
    count = lax.axis_size(axis)
    pairs = [(i, i + by) for i in range(count) if 0 <= i + by < count]
    return lax.ppermute(array, axis, pairs)


def swap(array, axis, bit):
    count = lax.axis_size(axis)
    return lax.ppermute(array, axis, [(i, i ^ bit) for i in range(count)])


def screen_block(block, screen_mask):
    aux_blocks, pair_blocks = screen_mask.shape
    aux_size = block.shape[0] // aux_blocks
    pair_size = block.shape[1] // pair_blocks
    expanded = jnp.repeat(jnp.repeat(screen_mask.astype(jnp.float32), aux_size, 0), pair_size, 1)
    return block * expanded


def product(left, right):
    return jnp.dot(left, right, precision=lax.Precision.HIGH, preferred_element_type=jnp.float32)


def contract_first(left, right):
    return lax.dot_general(
        left,
        right,
        (((0,), (0,)), ((), ())),
        precision=lax.Precision.HIGH,
        preferred_element_type=jnp.float32,
    )


def reduce_scatter_columns(partial, axis):
    index = lax.axis_index(axis)
    count = lax.axis_size(axis)
    current = partial
    bit = 1
    while bit < count:
        width = current.shape[1] // 2
        low, high = current[:, :width], current[:, width:]
        upper = (index // bit) % 2 == 1
        send = jnp.where(upper, low, high)
        keep = jnp.where(upper, high, low)
        current = keep + swap(send, axis, bit)
        bit *= 2
    return current


def all_gather_columns(share, axis):
    index = lax.axis_index(axis)
    count = lax.axis_size(axis)
    current = share
    bit = count // 2
    while bit >= 1:
        other = swap(current, axis, bit)
        upper = (index // bit) % 2 == 1
        current = jnp.where(
            upper,
            jnp.concatenate([other, current], axis=1),
            jnp.concatenate([current, other], axis=1),
        )
        bit //= 2
    return current


def gamma_over_aux(screened, densities):
    count = lax.axis_size("aux")
    index = lax.axis_index("aux")
    rows = densities.shape[0]

    def columns(block):
        start = jnp.clip(block, 0, count - 1) * rows
        return lax.dynamic_slice_in_dim(screened, start, rows, axis=1)

    gamma = product(columns(index), densities)
    from_left, from_right = densities, densities
    for step in range(count - 1):
        rightward = [(i, i + 1) for i in range(step, count - 1)]
        leftward = [(i + 1, i) for i in range(count - 1 - step)]
        from_left = lax.ppermute(from_left, "aux", rightward)
        from_right = lax.ppermute(from_right, "aux", leftward)
        gamma = gamma + product(columns(index - 1 - step), from_left)
        gamma = gamma + product(columns(index + 1 + step), from_right)
    return gamma


def reduce_over_aux(partial):
    count = lax.axis_size("aux")
    index = lax.axis_index("aux")
    rows = partial.shape[0] // count

    def block(owner):
        start = jnp.clip(owner, 0, count - 1) * rows
        return lax.dynamic_slice_in_dim(partial, start, rows, axis=0)

    to_right = jnp.zeros((rows, partial.shape[1]), partial.dtype)
    to_left = jnp.zeros((rows, partial.shape[1]), partial.dtype)
    for step in range(count - 1):
        rightward = [(i, i + 1) for i in range(min(step + 1, count - 1))]
        leftward = [(i + 1, i) for i in range(count - 2 - step, count - 1)]
        to_right = lax.ppermute(to_right + block(index + count - 1 - step), "aux", rightward)
        to_left = lax.ppermute(to_left + block(index - (count - 1) + step), "aux", leftward)
    return to_right + to_left + block(index)


def solve(right_side, transfer, diag_inverse, sub_factor):
    driving = product(diag_inverse, right_side)
    chain_length = lax.axis_size("aux")
    incoming = from_behind(driving, "aux", 1)
    for _ in range(chain_length - 2):
        incoming = from_behind(product(transfer, incoming) + driving, "aux", 1)
    solved = product(transfer, incoming) + driving
    source = product(sub_factor.T, product(diag_inverse.T, solved))
    back_map = transfer.T
    arriving = from_behind(source, "aux", -1)
    for _ in range(chain_length - 2):
        arriving = from_behind(product(back_map, arriving) + source, "aux", -1)
    return product(diag_inverse.T, solved - arriving)


SLICES = 2


def per_device(three_center, densities, screen_mask, diag_inverse, sub_factor):
    screened = screen_block(three_center, screen_mask)
    transfer = -product(diag_inverse, sub_factor)
    gamma_partial = gamma_over_aux(screened, densities)
    width = gamma_partial.shape[1] // SLICES
    results = []
    for part in range(SLICES):
        right_side = reduce_scatter_columns(gamma_partial[:, part * width:(part + 1) * width], "pair")
        coefficients = solve(right_side, transfer, diag_inverse, sub_factor)
        coeff_full = all_gather_columns(coefficients, "pair")
        partial = contract_first(screened, coeff_full)
        results.append(reduce_over_aux(partial))
    return jnp.concatenate(results, axis=1)


def solution(mesh):
    return jax.shard_map(
        per_device,
        mesh=mesh,
        in_specs=(
            P("aux", "pair"),
            P(("pair", "aux"), None),
            P("aux", "pair"),
            P("aux", None),
            P("aux", None),
        ),
        out_specs=P(("pair", "aux"), None),
        check_vma=False,
    )
```

```python
import jax
import jax.numpy as jnp
from jax import lax
from jax.sharding import PartitionSpec as P


def from_behind(array, axis, by):
    count = lax.axis_size(axis)
    pairs = [(i, i + by) for i in range(count) if 0 <= i + by < count]
    return lax.ppermute(array, axis, pairs)


def swap(array, axis, bit):
    count = lax.axis_size(axis)
    return lax.ppermute(array, axis, [(i, i ^ bit) for i in range(count)])


def screen_block(block, screen_mask):
    aux_blocks, pair_blocks = screen_mask.shape
    aux_size = block.shape[0] // aux_blocks
    pair_size = block.shape[1] // pair_blocks
    expanded = jnp.repeat(jnp.repeat(screen_mask.astype(jnp.float32), aux_size, 0), pair_size, 1)
    return block * expanded


def product(left, right):
    return jnp.dot(left, right, precision=lax.Precision.HIGH, preferred_element_type=jnp.float32)


def contract_first(left, right):
    return lax.dot_general(
        left,
        right,
        (((0,), (0,)), ((), ())),
        precision=lax.Precision.HIGH,
        preferred_element_type=jnp.float32,
    )


def reduce_scatter_columns(partial, axis):
    index = lax.axis_index(axis)
    count = lax.axis_size(axis)
    current = partial
    bit = 1
    while bit < count:
        width = current.shape[1] // 2
        low, high = current[:, :width], current[:, width:]
        upper = (index // bit) % 2 == 1
        send = jnp.where(upper, low, high)
        keep = jnp.where(upper, high, low)
        current = keep + swap(send, axis, bit)
        bit *= 2
    return current


def all_gather_columns(share, axis):
    index = lax.axis_index(axis)
    count = lax.axis_size(axis)
    current = share
    bit = count // 2
    while bit >= 1:
        other = swap(current, axis, bit)
        upper = (index // bit) % 2 == 1
        current = jnp.where(
            upper,
            jnp.concatenate([other, current], axis=1),
            jnp.concatenate([current, other], axis=1),
        )
        bit //= 2
    return current


def gamma_over_aux(screened, densities):
    count = lax.axis_size("aux")
    index = lax.axis_index("aux")
    rows = densities.shape[0]

    def columns(block):
        start = jnp.clip(block, 0, count - 1) * rows
        return lax.dynamic_slice_in_dim(screened, start, rows, axis=1)

    gamma = product(columns(index), densities)
    from_left, from_right = densities, densities
    for step in range(count - 1):
        rightward = [(i, i + 1) for i in range(step, count - 1)]
        leftward = [(i + 1, i) for i in range(count - 1 - step)]
        from_left = lax.ppermute(from_left, "aux", rightward)
        from_right = lax.ppermute(from_right, "aux", leftward)
        gamma = gamma + product(columns(index - 1 - step), from_left)
        gamma = gamma + product(columns(index + 1 + step), from_right)
    return gamma


def reduce_over_aux(partial):
    count = lax.axis_size("aux")
    index = lax.axis_index("aux")
    rows = partial.shape[0] // count

    def block(owner):
        start = jnp.clip(owner, 0, count - 1) * rows
        return lax.dynamic_slice_in_dim(partial, start, rows, axis=0)

    to_right = jnp.zeros((rows, partial.shape[1]), partial.dtype)
    to_left = jnp.zeros((rows, partial.shape[1]), partial.dtype)
    for step in range(count - 1):
        rightward = [(i, i + 1) for i in range(min(step + 1, count - 1))]
        leftward = [(i + 1, i) for i in range(count - 2 - step, count - 1)]
        to_right = lax.ppermute(to_right + block(index + count - 1 - step), "aux", rightward)
        to_left = lax.ppermute(to_left + block(index - (count - 1) + step), "aux", leftward)
    return to_right + to_left + block(index)


def solve(right_side, transfer, diag_inverse, sub_factor):
    driving = product(diag_inverse, right_side)
    chain_length = lax.axis_size("aux")
    incoming = from_behind(driving, "aux", 1)
    for _ in range(chain_length - 2):
        incoming = from_behind(product(transfer, incoming) + driving, "aux", 1)
    solved = product(transfer, incoming) + driving
    source = product(sub_factor.T, product(diag_inverse.T, solved))
    back_map = transfer.T
    arriving = from_behind(source, "aux", -1)
    for _ in range(chain_length - 2):
        arriving = from_behind(product(back_map, arriving) + source, "aux", -1)
    return product(diag_inverse.T, solved - arriving)


SLICES = 2


def per_device(three_center, densities, screen_mask, diag_inverse, sub_factor):
    screened = screen_block(three_center, screen_mask)
    transfer = -product(diag_inverse, sub_factor)
    gamma_partial = gamma_over_aux(screened, densities)
    width = gamma_partial.shape[1] // SLICES
    parts = range(SLICES)
    right_sides = [reduce_scatter_columns(gamma_partial[:, p * width:(p + 1) * width], "pair") for p in parts]
    coefficients = [solve(r, transfer, diag_inverse, sub_factor) for r in right_sides]
    coeff_full = [all_gather_columns(c, "pair") for c in coefficients]
    partials = [contract_first(screened, c) for c in coeff_full]
    return jnp.concatenate([reduce_over_aux(p) for p in partials], axis=1)


def solution(mesh):
    return jax.shard_map(
        per_device,
        mesh=mesh,
        in_specs=(
            P("aux", "pair"),
            P(("pair", "aux"), None),
            P("aux", "pair"),
            P("aux", None),
            P("aux", None),
        ),
        out_specs=P(("pair", "aux"), None),
        check_vma=False,
    )
```

```python
import jax
import jax.numpy as jnp
from jax import lax
from jax.sharding import PartitionSpec as P


def from_behind(array, axis, by):
    count = lax.axis_size(axis)
    pairs = [(i, i + by) for i in range(count) if 0 <= i + by < count]
    return lax.ppermute(array, axis, pairs)


def swap(array, axis, bit):
    count = lax.axis_size(axis)
    return lax.ppermute(array, axis, [(i, i ^ bit) for i in range(count)])


def screen_block(block, screen_mask):
    aux_blocks, pair_blocks = screen_mask.shape
    aux_size = block.shape[0] // aux_blocks
    pair_size = block.shape[1] // pair_blocks
    expanded = jnp.repeat(jnp.repeat(screen_mask.astype(jnp.float32), aux_size, 0), pair_size, 1)
    return block * expanded


def product(left, right):
    return jnp.dot(left, right, precision=lax.Precision.HIGH, preferred_element_type=jnp.float32)


def contract_first(left, right):
    return lax.dot_general(
        left,
        right,
        (((0,), (0,)), ((), ())),
        precision=lax.Precision.HIGH,
        preferred_element_type=jnp.float32,
    )


def reduce_scatter_columns(partial, axis):
    index = lax.axis_index(axis)
    count = lax.axis_size(axis)
    current = partial
    bit = 1
    while bit < count:
        width = current.shape[1] // 2
        low, high = current[:, :width], current[:, width:]
        upper = (index // bit) % 2 == 1
        send = jnp.where(upper, low, high)
        keep = jnp.where(upper, high, low)
        current = keep + swap(send, axis, bit)
        bit *= 2
    return current


def all_gather_columns(share, axis):
    index = lax.axis_index(axis)
    count = lax.axis_size(axis)
    current = share
    bit = count // 2
    while bit >= 1:
        other = swap(current, axis, bit)
        upper = (index // bit) % 2 == 1
        current = jnp.where(
            upper,
            jnp.concatenate([other, current], axis=1),
            jnp.concatenate([current, other], axis=1),
        )
        bit //= 2
    return current


def gamma_over_aux(screened, densities):
    count = lax.axis_size("aux")
    index = lax.axis_index("aux")
    rows = densities.shape[0]

    def columns(block):
        start = jnp.clip(block, 0, count - 1) * rows
        return lax.dynamic_slice_in_dim(screened, start, rows, axis=1)

    gamma = product(columns(index), densities)
    from_left, from_right = densities, densities
    for step in range(count - 1):
        rightward = [(i, i + 1) for i in range(step, count - 1)]
        leftward = [(i + 1, i) for i in range(count - 1 - step)]
        from_left = lax.ppermute(from_left, "aux", rightward)
        from_right = lax.ppermute(from_right, "aux", leftward)
        gamma = gamma + product(columns(index - 1 - step), from_left)
        gamma = gamma + product(columns(index + 1 + step), from_right)
    return gamma


def reduce_over_aux(partial):
    count = lax.axis_size("aux")
    index = lax.axis_index("aux")
    rows = partial.shape[0] // count

    def block(owner):
        start = jnp.clip(owner, 0, count - 1) * rows
        return lax.dynamic_slice_in_dim(partial, start, rows, axis=0)

    to_right = jnp.zeros((rows, partial.shape[1]), partial.dtype)
    to_left = jnp.zeros((rows, partial.shape[1]), partial.dtype)
    for step in range(count - 1):
        rightward = [(i, i + 1) for i in range(min(step + 1, count - 1))]
        leftward = [(i + 1, i) for i in range(count - 2 - step, count - 1)]
        to_right = lax.ppermute(to_right + block(index + count - 1 - step), "aux", rightward)
        to_left = lax.ppermute(to_left + block(index - (count - 1) + step), "aux", leftward)
    return to_right + to_left + block(index)


def solve(right_side, transfer, diag_inverse, sub_factor):
    driving = product(diag_inverse, right_side)
    chain_length = lax.axis_size("aux")
    incoming = jnp.zeros_like(driving)
    for turn in range(chain_length - 1):
        value = driving if turn == 0 else product(transfer, incoming) + driving
        incoming = incoming + lax.ppermute(value, "aux", [(turn, turn + 1)])
    solved = product(transfer, incoming) + driving
    source = product(sub_factor.T, product(diag_inverse.T, solved))
    back_map = transfer.T
    arriving = jnp.zeros_like(driving)
    for turn in range(chain_length - 1):
        sender = chain_length - 1 - turn
        value = source if turn == 0 else product(back_map, arriving) + source
        arriving = arriving + lax.ppermute(value, "aux", [(sender, sender - 1)])
    return product(diag_inverse.T, solved - arriving)


SLICES = 2


def per_device(three_center, densities, screen_mask, diag_inverse, sub_factor):
    screened = screen_block(three_center, screen_mask)
    transfer = -product(diag_inverse, sub_factor)
    gamma_partial = gamma_over_aux(screened, densities)
    width = gamma_partial.shape[1] // SLICES
    results = []
    for part in range(SLICES):
        right_side = reduce_scatter_columns(gamma_partial[:, part * width:(part + 1) * width], "pair")
        coefficients = solve(right_side, transfer, diag_inverse, sub_factor)
        coeff_full = all_gather_columns(coefficients, "pair")
        partial = contract_first(screened, coeff_full)
        results.append(reduce_over_aux(partial))
    return jnp.concatenate(results, axis=1)


def solution(mesh):
    return jax.shard_map(
        per_device,
        mesh=mesh,
        in_specs=(
            P("aux", "pair"),
            P(("pair", "aux"), None),
            P("aux", "pair"),
            P("aux", None),
            P("aux", None),
        ),
        out_specs=P(("pair", "aux"), None),
        check_vma=False,
    )
```

```python
import jax
import jax.numpy as jnp
from jax import lax
from jax.sharding import PartitionSpec as P


def from_behind(array, axis, by):
    count = lax.axis_size(axis)
    pairs = [(i, i + by) for i in range(count) if 0 <= i + by < count]
    return lax.ppermute(array, axis, pairs)


def swap(array, axis, bit):
    count = lax.axis_size(axis)
    return lax.ppermute(array, axis, [(i, i ^ bit) for i in range(count)])


def screen_block(block, screen_mask):
    aux_blocks, pair_blocks = screen_mask.shape
    aux_size = block.shape[0] // aux_blocks
    pair_size = block.shape[1] // pair_blocks
    expanded = jnp.repeat(jnp.repeat(screen_mask.astype(jnp.float32), aux_size, 0), pair_size, 1)
    return block * expanded


def product(left, right):
    return jnp.dot(left, right, precision=lax.Precision.HIGH, preferred_element_type=jnp.float32)


def contract_first(left, right):
    return lax.dot_general(
        left,
        right,
        (((0,), (0,)), ((), ())),
        precision=lax.Precision.HIGH,
        preferred_element_type=jnp.float32,
    )


def reduce_scatter_columns(partial, axis):
    index = lax.axis_index(axis)
    count = lax.axis_size(axis)
    current = partial
    bit = 1
    while bit < count:
        width = current.shape[1] // 2
        low, high = current[:, :width], current[:, width:]
        upper = (index // bit) % 2 == 1
        send = jnp.where(upper, low, high)
        keep = jnp.where(upper, high, low)
        current = keep + swap(send, axis, bit)
        bit *= 2
    return current


def all_gather_columns(share, axis):
    index = lax.axis_index(axis)
    count = lax.axis_size(axis)
    current = share
    bit = count // 2
    while bit >= 1:
        other = swap(current, axis, bit)
        upper = (index // bit) % 2 == 1
        current = jnp.where(
            upper,
            jnp.concatenate([other, current], axis=1),
            jnp.concatenate([current, other], axis=1),
        )
        bit //= 2
    return current


def gamma_over_aux(screened, densities):
    count = lax.axis_size("aux")
    index = lax.axis_index("aux")
    rows = densities.shape[0]

    def columns(block):
        start = jnp.clip(block, 0, count - 1) * rows
        return lax.dynamic_slice_in_dim(screened, start, rows, axis=1)

    gamma = product(columns(index), densities)
    from_left, from_right = densities, densities
    for step in range(count - 1):
        rightward = [(i, i + 1) for i in range(step, count - 1)]
        leftward = [(i + 1, i) for i in range(count - 1 - step)]
        from_left = lax.ppermute(from_left, "aux", rightward)
        from_right = lax.ppermute(from_right, "aux", leftward)
        gamma = gamma + product(columns(index - 1 - step), from_left)
        gamma = gamma + product(columns(index + 1 + step), from_right)
    return gamma


def reduce_over_aux(partial):
    count = lax.axis_size("aux")
    index = lax.axis_index("aux")
    rows = partial.shape[0] // count

    def block(owner):
        start = jnp.clip(owner, 0, count - 1) * rows
        return lax.dynamic_slice_in_dim(partial, start, rows, axis=0)

    to_right = jnp.zeros((rows, partial.shape[1]), partial.dtype)
    to_left = jnp.zeros((rows, partial.shape[1]), partial.dtype)
    for step in range(count - 1):
        rightward = [(i, i + 1) for i in range(min(step + 1, count - 1))]
        leftward = [(i + 1, i) for i in range(count - 2 - step, count - 1)]
        to_right = lax.ppermute(to_right + block(index + count - 1 - step), "aux", rightward)
        to_left = lax.ppermute(to_left + block(index - (count - 1) + step), "aux", leftward)
    return to_right + to_left + block(index)


def solve(right_side, transfer, diag_inverse, sub_factor):
    driving = product(diag_inverse, right_side)
    chain_length = lax.axis_size("aux")
    incoming = jnp.zeros_like(driving)
    for turn in range(chain_length - 1):
        value = driving if turn == 0 else product(transfer, incoming) + driving
        incoming = incoming + lax.ppermute(value, "aux", [(turn, turn + 1)])
    solved = product(transfer, incoming) + driving
    source = product(sub_factor.T, product(diag_inverse.T, solved))
    back_map = transfer.T
    arriving = jnp.zeros_like(driving)
    for turn in range(chain_length - 1):
        sender = chain_length - 1 - turn
        value = source if turn == 0 else product(back_map, arriving) + source
        arriving = arriving + lax.ppermute(value, "aux", [(sender, sender - 1)])
    return product(diag_inverse.T, solved - arriving)


SLICES = 1


def per_device(three_center, densities, screen_mask, diag_inverse, sub_factor):
    screened = screen_block(three_center, screen_mask)
    transfer = -product(diag_inverse, sub_factor)
    gamma_partial = gamma_over_aux(screened, densities)
    width = gamma_partial.shape[1] // SLICES
    results = []
    for part in range(SLICES):
        right_side = reduce_scatter_columns(gamma_partial[:, part * width:(part + 1) * width], "pair")
        coefficients = solve(right_side, transfer, diag_inverse, sub_factor)
        coeff_full = all_gather_columns(coefficients, "pair")
        partial = contract_first(screened, coeff_full)
        results.append(reduce_over_aux(partial))
    return jnp.concatenate(results, axis=1)


def solution(mesh):
    return jax.shard_map(
        per_device,
        mesh=mesh,
        in_specs=(
            P("aux", "pair"),
            P(("pair", "aux"), None),
            P("aux", "pair"),
            P("aux", None),
            P("aux", None),
        ),
        out_specs=P(("pair", "aux"), None),
        check_vma=False,
    )
```

```python
import jax
import jax.numpy as jnp
from jax import lax
from jax.sharding import PartitionSpec as P


def from_behind(array, axis, by):
    count = lax.axis_size(axis)
    pairs = [(i, i + by) for i in range(count) if 0 <= i + by < count]
    return lax.ppermute(array, axis, pairs)


def pairwise(array, axis, pairs):
    received = [lax.ppermute(array, axis, [pair]) for pair in pairs]
    total = received[0]
    for more in received[1:]:
        total = total + more
    return total


def swap(array, axis, bit):
    count = lax.axis_size(axis)
    return lax.ppermute(array, axis, [(i, i ^ bit) for i in range(count)])


def screen_block(block, screen_mask):
    aux_blocks, pair_blocks = screen_mask.shape
    aux_size = block.shape[0] // aux_blocks
    pair_size = block.shape[1] // pair_blocks
    expanded = jnp.repeat(jnp.repeat(screen_mask.astype(jnp.float32), aux_size, 0), pair_size, 1)
    return block * expanded


def product(left, right):
    return jnp.dot(left, right, precision=lax.Precision.HIGH, preferred_element_type=jnp.float32)


def contract_first(left, right):
    return lax.dot_general(
        left,
        right,
        (((0,), (0,)), ((), ())),
        precision=lax.Precision.HIGH,
        preferred_element_type=jnp.float32,
    )


def reduce_scatter_columns(partial, axis):
    index = lax.axis_index(axis)
    count = lax.axis_size(axis)
    current = partial
    bit = 1
    while bit < count:
        width = current.shape[1] // 2
        low, high = current[:, :width], current[:, width:]
        upper = (index // bit) % 2 == 1
        send = jnp.where(upper, low, high)
        keep = jnp.where(upper, high, low)
        current = keep + swap(send, axis, bit)
        bit *= 2
    return current


def all_gather_columns(share, axis):
    index = lax.axis_index(axis)
    count = lax.axis_size(axis)
    current = share
    bit = count // 2
    while bit >= 1:
        other = swap(current, axis, bit)
        upper = (index // bit) % 2 == 1
        current = jnp.where(
            upper,
            jnp.concatenate([other, current], axis=1),
            jnp.concatenate([current, other], axis=1),
        )
        bit //= 2
    return current


def gamma_over_aux(screened, densities):
    count = lax.axis_size("aux")
    index = lax.axis_index("aux")
    rows = densities.shape[0]

    def columns(block):
        start = jnp.clip(block, 0, count - 1) * rows
        return lax.dynamic_slice_in_dim(screened, start, rows, axis=1)

    gamma = product(columns(index), densities)
    from_left, from_right = densities, densities
    for step in range(count - 1):
        rightward = [(i, i + 1) for i in range(step, count - 1)]
        leftward = [(i + 1, i) for i in range(count - 1 - step)]
        from_left = pairwise(from_left, "aux", rightward)
        from_right = pairwise(from_right, "aux", leftward)
        gamma = gamma + product(columns(index - 1 - step), from_left)
        gamma = gamma + product(columns(index + 1 + step), from_right)
    return gamma


def reduce_over_aux(partial):
    count = lax.axis_size("aux")
    index = lax.axis_index("aux")
    rows = partial.shape[0] // count

    def block(owner):
        start = jnp.clip(owner, 0, count - 1) * rows
        return lax.dynamic_slice_in_dim(partial, start, rows, axis=0)

    to_right = jnp.zeros((rows, partial.shape[1]), partial.dtype)
    to_left = jnp.zeros((rows, partial.shape[1]), partial.dtype)
    for step in range(count - 1):
        rightward = [(i, i + 1) for i in range(min(step + 1, count - 1))]
        leftward = [(i + 1, i) for i in range(count - 2 - step, count - 1)]
        to_right = pairwise(to_right + block(index + count - 1 - step), "aux", rightward)
        to_left = pairwise(to_left + block(index - (count - 1) + step), "aux", leftward)
    return to_right + to_left + block(index)


def solve(right_side, transfer, diag_inverse, sub_factor):
    driving = product(diag_inverse, right_side)
    chain_length = lax.axis_size("aux")
    incoming = jnp.zeros_like(driving)
    for turn in range(chain_length - 1):
        value = driving if turn == 0 else product(transfer, incoming) + driving
        incoming = incoming + lax.ppermute(value, "aux", [(turn, turn + 1)])
    solved = product(transfer, incoming) + driving
    source = product(sub_factor.T, product(diag_inverse.T, solved))
    back_map = transfer.T
    arriving = jnp.zeros_like(driving)
    for turn in range(chain_length - 1):
        sender = chain_length - 1 - turn
        value = source if turn == 0 else product(back_map, arriving) + source
        arriving = arriving + lax.ppermute(value, "aux", [(sender, sender - 1)])
    return product(diag_inverse.T, solved - arriving)


SLICES = 2


def per_device(three_center, densities, screen_mask, diag_inverse, sub_factor):
    screened = screen_block(three_center, screen_mask)
    transfer = -product(diag_inverse, sub_factor)
    gamma_partial = gamma_over_aux(screened, densities)
    width = gamma_partial.shape[1] // SLICES
    results = []
    for part in range(SLICES):
        right_side = reduce_scatter_columns(gamma_partial[:, part * width:(part + 1) * width], "pair")
        coefficients = solve(right_side, transfer, diag_inverse, sub_factor)
        coeff_full = all_gather_columns(coefficients, "pair")
        partial = contract_first(screened, coeff_full)
        results.append(reduce_over_aux(partial))
    return jnp.concatenate(results, axis=1)


def solution(mesh):
    return jax.shard_map(
        per_device,
        mesh=mesh,
        in_specs=(
            P("aux", "pair"),
            P(("pair", "aux"), None),
            P("aux", "pair"),
            P("aux", None),
            P("aux", None),
        ),
        out_specs=P(("pair", "aux"), None),
        check_vma=False,
    )
```

```python
import jax
import jax.numpy as jnp
from jax import lax
from jax.sharding import PartitionSpec as P


def from_behind(array, axis, by):
    count = lax.axis_size(axis)
    pairs = [(i, i + by) for i in range(count) if 0 <= i + by < count]
    return lax.ppermute(array, axis, pairs)


def swap(array, axis, bit):
    count = lax.axis_size(axis)
    return lax.ppermute(array, axis, [(i, i ^ bit) for i in range(count)])


def screen_block(block, screen_mask):
    aux_blocks, pair_blocks = screen_mask.shape
    aux_size = block.shape[0] // aux_blocks
    pair_size = block.shape[1] // pair_blocks
    expanded = jnp.repeat(jnp.repeat(screen_mask.astype(jnp.float32), aux_size, 0), pair_size, 1)
    return block * expanded


def product(left, right):
    return jnp.dot(left, right, precision=lax.Precision.HIGH, preferred_element_type=jnp.float32)


def contract_first(left, right):
    return lax.dot_general(
        left,
        right,
        (((0,), (0,)), ((), ())),
        precision=lax.Precision.HIGH,
        preferred_element_type=jnp.float32,
    )


def reduce_scatter_columns(partial, axis):
    index = lax.axis_index(axis)
    count = lax.axis_size(axis)
    current = partial
    bit = 1
    while bit < count:
        width = current.shape[1] // 2
        low, high = current[:, :width], current[:, width:]
        upper = (index // bit) % 2 == 1
        send = jnp.where(upper, low, high)
        keep = jnp.where(upper, high, low)
        current = keep + swap(send, axis, bit)
        bit *= 2
    return current


def all_gather_columns(share, axis):
    index = lax.axis_index(axis)
    count = lax.axis_size(axis)
    current = share
    bit = count // 2
    while bit >= 1:
        other = swap(current, axis, bit)
        upper = (index // bit) % 2 == 1
        current = jnp.where(
            upper,
            jnp.concatenate([other, current], axis=1),
            jnp.concatenate([current, other], axis=1),
        )
        bit //= 2
    return current


def gamma_over_aux(screened, densities):
    count = lax.axis_size("aux")
    index = lax.axis_index("aux")
    rows = densities.shape[0]

    def columns(block):
        start = jnp.clip(block, 0, count - 1) * rows
        return lax.dynamic_slice_in_dim(screened, start, rows, axis=1)

    gamma = product(columns(index), densities)
    from_left, from_right = densities, densities
    for step in range(count - 1):
        rightward = [(i, i + 1) for i in range(step, count - 1)]
        leftward = [(i + 1, i) for i in range(count - 1 - step)]
        from_left = lax.ppermute(from_left, "aux", rightward)
        from_right = lax.ppermute(from_right, "aux", leftward)
        gamma = gamma + product(columns(index - 1 - step), from_left)
        gamma = gamma + product(columns(index + 1 + step), from_right)
    return gamma


def reduce_over_aux(partial):
    count = lax.axis_size("aux")
    index = lax.axis_index("aux")
    rows = partial.shape[0] // count

    def block(owner):
        start = jnp.clip(owner, 0, count - 1) * rows
        return lax.dynamic_slice_in_dim(partial, start, rows, axis=0)

    to_right = jnp.zeros((rows, partial.shape[1]), partial.dtype)
    to_left = jnp.zeros((rows, partial.shape[1]), partial.dtype)
    for step in range(count - 1):
        rightward = [(i, i + 1) for i in range(min(step + 1, count - 1))]
        leftward = [(i + 1, i) for i in range(count - 2 - step, count - 1)]
        to_right = lax.ppermute(to_right + block(index + count - 1 - step), "aux", rightward)
        to_left = lax.ppermute(to_left + block(index - (count - 1) + step), "aux", leftward)
    return to_right + to_left + block(index)


def solve(right_side, transfer, diag_inverse, sub_factor):
    driving = product(diag_inverse, right_side)
    chain_length = lax.axis_size("aux")
    incoming = jnp.zeros_like(driving)
    for turn in range(chain_length - 1):
        value = driving if turn == 0 else product(transfer, incoming) + driving
        incoming = incoming + lax.ppermute(value, "aux", [(turn, turn + 1)])
    solved = product(transfer, incoming) + driving
    source = product(sub_factor.T, product(diag_inverse.T, solved))
    back_map = transfer.T
    arriving = jnp.zeros_like(driving)
    for turn in range(chain_length - 1):
        sender = chain_length - 1 - turn
        value = source if turn == 0 else product(back_map, arriving) + source
        arriving = arriving + lax.ppermute(value, "aux", [(sender, sender - 1)])
    return product(diag_inverse.T, solved - arriving)


SLICES = 2


def per_device(three_center, densities, screen_mask, diag_inverse, sub_factor):
    screened = screen_block(three_center, screen_mask)
    transfer = -product(diag_inverse, sub_factor)
    gamma_partial = gamma_over_aux(screened, densities)
    width = gamma_partial.shape[1] // SLICES
    results = []
    for part in range(SLICES):
        right_side = reduce_scatter_columns(gamma_partial[:, part * width:(part + 1) * width], "pair")
        half = right_side.shape[1] // 2
        coefficients = jnp.concatenate(
            [solve(right_side[:, :half], transfer, diag_inverse, sub_factor),
             solve(right_side[:, half:], transfer, diag_inverse, sub_factor)], axis=1)
        coeff_full = all_gather_columns(coefficients, "pair")
        partial = contract_first(screened, coeff_full)
        results.append(reduce_over_aux(partial))
    return jnp.concatenate(results, axis=1)


def solution(mesh):
    return jax.shard_map(
        per_device,
        mesh=mesh,
        in_specs=(
            P("aux", "pair"),
            P(("pair", "aux"), None),
            P("aux", "pair"),
            P("aux", None),
            P("aux", None),
        ),
        out_specs=P(("pair", "aux"), None),
        check_vma=False,
    )
```

```python
import jax
import jax.numpy as jnp
from jax import lax
from jax.sharding import PartitionSpec as P


def from_behind(array, axis, by):
    count = lax.axis_size(axis)
    pairs = [(i, i + by) for i in range(count) if 0 <= i + by < count]
    return lax.ppermute(array, axis, pairs)


def swap(array, axis, bit):
    count = lax.axis_size(axis)
    return lax.ppermute(array, axis, [(i, i ^ bit) for i in range(count)])


def screen_block(block, screen_mask):
    aux_blocks, pair_blocks = screen_mask.shape
    aux_size = block.shape[0] // aux_blocks
    pair_size = block.shape[1] // pair_blocks
    expanded = jnp.repeat(jnp.repeat(screen_mask.astype(jnp.float32), aux_size, 0), pair_size, 1)
    return block * expanded


def product(left, right):
    return jnp.dot(left, right, precision=lax.Precision.HIGH, preferred_element_type=jnp.float32)


def contract_first(left, right):
    return lax.dot_general(
        left,
        right,
        (((0,), (0,)), ((), ())),
        precision=lax.Precision.HIGH,
        preferred_element_type=jnp.float32,
    )


def reduce_scatter_columns(partial, axis):
    index = lax.axis_index(axis)
    count = lax.axis_size(axis)
    current = partial
    bit = 1
    while bit < count:
        width = current.shape[1] // 2
        upper = (index // bit) % 2
        send = lax.dynamic_slice_in_dim(current, (1 - upper) * width, width, axis=1)
        keep = lax.dynamic_slice_in_dim(current, upper * width, width, axis=1)
        current = keep + swap(send, axis, bit)
        bit *= 2
    return current


def all_gather_columns(share, axis):
    index = lax.axis_index(axis)
    count = lax.axis_size(axis)
    current = share
    bit = count // 2
    while bit >= 1:
        other = swap(current, axis, bit)
        upper = (index // bit) % 2 == 1
        current = jnp.where(
            upper,
            jnp.concatenate([other, current], axis=1),
            jnp.concatenate([current, other], axis=1),
        )
        bit //= 2
    return current


def gamma_over_aux(screened, densities):
    count = lax.axis_size("aux")
    index = lax.axis_index("aux")
    rows = densities.shape[0]

    def columns(block):
        start = jnp.clip(block, 0, count - 1) * rows
        return lax.dynamic_slice_in_dim(screened, start, rows, axis=1)

    gamma = product(columns(index), densities)
    from_left, from_right = densities, densities
    for step in range(count - 1):
        rightward = [(i, i + 1) for i in range(step, count - 1)]
        leftward = [(i + 1, i) for i in range(count - 1 - step)]
        from_left = lax.ppermute(from_left, "aux", rightward)
        from_right = lax.ppermute(from_right, "aux", leftward)
        gamma = gamma + product(columns(index - 1 - step), from_left)
        gamma = gamma + product(columns(index + 1 + step), from_right)
    return gamma


def reduce_over_aux(partial):
    count = lax.axis_size("aux")
    index = lax.axis_index("aux")
    rows = partial.shape[0] // count

    def block(owner):
        start = jnp.clip(owner, 0, count - 1) * rows
        return lax.dynamic_slice_in_dim(partial, start, rows, axis=0)

    to_right = jnp.zeros((rows, partial.shape[1]), partial.dtype)
    to_left = jnp.zeros((rows, partial.shape[1]), partial.dtype)
    for step in range(count - 1):
        rightward = [(i, i + 1) for i in range(min(step + 1, count - 1))]
        leftward = [(i + 1, i) for i in range(count - 2 - step, count - 1)]
        to_right = lax.ppermute(to_right + block(index + count - 1 - step), "aux", rightward)
        to_left = lax.ppermute(to_left + block(index - (count - 1) + step), "aux", leftward)
    return to_right + to_left + block(index)


def solve(right_side, transfer, diag_inverse, sub_factor):
    driving = product(diag_inverse, right_side)
    chain_length = lax.axis_size("aux")
    incoming = jnp.zeros_like(driving)
    for turn in range(chain_length - 1):
        value = driving if turn == 0 else product(transfer, incoming) + driving
        incoming = incoming + lax.ppermute(value, "aux", [(turn, turn + 1)])
    solved = product(transfer, incoming) + driving
    source = product(sub_factor.T, product(diag_inverse.T, solved))
    back_map = transfer.T
    arriving = jnp.zeros_like(driving)
    for turn in range(chain_length - 1):
        sender = chain_length - 1 - turn
        value = source if turn == 0 else product(back_map, arriving) + source
        arriving = arriving + lax.ppermute(value, "aux", [(sender, sender - 1)])
    return product(diag_inverse.T, solved - arriving)


SLICES = 2


def per_device(three_center, densities, screen_mask, diag_inverse, sub_factor):
    screened = screen_block(three_center, screen_mask)
    transfer = -product(diag_inverse, sub_factor)
    gamma_partial = gamma_over_aux(screened, densities)
    width = gamma_partial.shape[1] // SLICES
    results = []
    for part in range(SLICES):
        right_side = reduce_scatter_columns(gamma_partial[:, part * width:(part + 1) * width], "pair")
        coefficients = solve(right_side, transfer, diag_inverse, sub_factor)
        coeff_full = all_gather_columns(coefficients, "pair")
        partial = contract_first(screened, coeff_full)
        results.append(reduce_over_aux(partial))
    return jnp.concatenate(results, axis=1)


def solution(mesh):
    return jax.shard_map(
        per_device,
        mesh=mesh,
        in_specs=(
            P("aux", "pair"),
            P(("pair", "aux"), None),
            P("aux", "pair"),
            P("aux", None),
            P("aux", None),
        ),
        out_specs=P(("pair", "aux"), None),
        check_vma=False,
    )
```

```python
import jax
import jax.numpy as jnp
from jax import lax
from jax.sharding import PartitionSpec as P


def from_behind(array, axis, by):
    count = lax.axis_size(axis)
    pairs = [(i, i + by) for i in range(count) if 0 <= i + by < count]
    return lax.ppermute(array, axis, pairs)


def swap(array, axis, bit):
    count = lax.axis_size(axis)
    return lax.ppermute(array, axis, [(i, i ^ bit) for i in range(count)])


def screen_block(block, screen_mask):
    aux_blocks, pair_blocks = screen_mask.shape
    aux_size = block.shape[0] // aux_blocks
    pair_size = block.shape[1] // pair_blocks
    expanded = jnp.repeat(jnp.repeat(screen_mask.astype(jnp.float32), aux_size, 0), pair_size, 1)
    return block * expanded


def product(left, right):
    return jnp.dot(left, right, precision=lax.Precision.HIGH, preferred_element_type=jnp.float32)


def contract_first(left, right):
    return lax.dot_general(
        left,
        right,
        (((0,), (0,)), ((), ())),
        precision=lax.Precision.HIGH,
        preferred_element_type=jnp.float32,
    )


def reduce_scatter_columns(partial, axis):
    index = lax.axis_index(axis)
    count = lax.axis_size(axis)
    current = partial
    bit = 1
    while bit < count:
        width = current.shape[1] // 2
        low, high = current[:, :width], current[:, width:]
        upper = (index // bit) % 2 == 1
        send = jnp.where(upper, low, high)
        keep = jnp.where(upper, high, low)
        current = keep + swap(send, axis, bit)
        bit *= 2
    return current


def all_gather_columns(share, axis):
    index = lax.axis_index(axis)
    count = lax.axis_size(axis)
    current = share
    bit = count // 2
    while bit >= 1:
        other = swap(current, axis, bit)
        upper = (index // bit) % 2
        width = current.shape[1]
        joined = jnp.zeros((current.shape[0], 2 * width), current.dtype)
        joined = lax.dynamic_update_slice_in_dim(joined, current, upper * width, axis=1)
        current = lax.dynamic_update_slice_in_dim(joined, other, (1 - upper) * width, axis=1)
        bit //= 2
    return current


def gamma_over_aux(screened, densities):
    count = lax.axis_size("aux")
    index = lax.axis_index("aux")
    rows = densities.shape[0]

    def columns(block):
        start = jnp.clip(block, 0, count - 1) * rows
        return lax.dynamic_slice_in_dim(screened, start, rows, axis=1)

    gamma = product(columns(index), densities)
    from_left, from_right = densities, densities
    for step in range(count - 1):
        rightward = [(i, i + 1) for i in range(step, count - 1)]
        leftward = [(i + 1, i) for i in range(count - 1 - step)]
        from_left = lax.ppermute(from_left, "aux", rightward)
        from_right = lax.ppermute(from_right, "aux", leftward)
        gamma = gamma + product(columns(index - 1 - step), from_left)
        gamma = gamma + product(columns(index + 1 + step), from_right)
    return gamma


def reduce_over_aux(partial):
    count = lax.axis_size("aux")
    index = lax.axis_index("aux")
    rows = partial.shape[0] // count

    def block(owner):
        start = jnp.clip(owner, 0, count - 1) * rows
        return lax.dynamic_slice_in_dim(partial, start, rows, axis=0)

    to_right = jnp.zeros((rows, partial.shape[1]), partial.dtype)
    to_left = jnp.zeros((rows, partial.shape[1]), partial.dtype)
    for step in range(count - 1):
        rightward = [(i, i + 1) for i in range(min(step + 1, count - 1))]
        leftward = [(i + 1, i) for i in range(count - 2 - step, count - 1)]
        to_right = lax.ppermute(to_right + block(index + count - 1 - step), "aux", rightward)
        to_left = lax.ppermute(to_left + block(index - (count - 1) + step), "aux", leftward)
    return to_right + to_left + block(index)


def solve(right_side, transfer, diag_inverse, sub_factor):
    driving = product(diag_inverse, right_side)
    chain_length = lax.axis_size("aux")
    incoming = jnp.zeros_like(driving)
    for turn in range(chain_length - 1):
        value = driving if turn == 0 else product(transfer, incoming) + driving
        incoming = incoming + lax.ppermute(value, "aux", [(turn, turn + 1)])
    solved = product(transfer, incoming) + driving
    source = product(sub_factor.T, product(diag_inverse.T, solved))
    back_map = transfer.T
    arriving = jnp.zeros_like(driving)
    for turn in range(chain_length - 1):
        sender = chain_length - 1 - turn
        value = source if turn == 0 else product(back_map, arriving) + source
        arriving = arriving + lax.ppermute(value, "aux", [(sender, sender - 1)])
    return product(diag_inverse.T, solved - arriving)


SLICES = 2


def per_device(three_center, densities, screen_mask, diag_inverse, sub_factor):
    screened = screen_block(three_center, screen_mask)
    transfer = -product(diag_inverse, sub_factor)
    gamma_partial = gamma_over_aux(screened, densities)
    width = gamma_partial.shape[1] // SLICES
    results = []
    for part in range(SLICES):
        right_side = reduce_scatter_columns(gamma_partial[:, part * width:(part + 1) * width], "pair")
        coefficients = solve(right_side, transfer, diag_inverse, sub_factor)
        coeff_full = all_gather_columns(coefficients, "pair")
        partial = contract_first(screened, coeff_full)
        results.append(reduce_over_aux(partial))
    return jnp.concatenate(results, axis=1)


def solution(mesh):
    return jax.shard_map(
        per_device,
        mesh=mesh,
        in_specs=(
            P("aux", "pair"),
            P(("pair", "aux"), None),
            P("aux", "pair"),
            P("aux", None),
            P("aux", None),
        ),
        out_specs=P(("pair", "aux"), None),
        check_vma=False,
    )
```

```python
import jax
import jax.numpy as jnp
from jax import lax
from jax.sharding import PartitionSpec as P


def from_behind(array, axis, by):
    count = lax.axis_size(axis)
    pairs = [(i, i + by) for i in range(count) if 0 <= i + by < count]
    return lax.ppermute(array, axis, pairs)


def swap(array, axis, bit):
    count = lax.axis_size(axis)
    return lax.ppermute(array, axis, [(i, i ^ bit) for i in range(count)])


def screen_block(block, screen_mask):
    aux_blocks, pair_blocks = screen_mask.shape
    aux_size = block.shape[0] // aux_blocks
    pair_size = block.shape[1] // pair_blocks
    expanded = jnp.repeat(jnp.repeat(screen_mask.astype(jnp.float32), aux_size, 0), pair_size, 1)
    return block * expanded


def product(left, right):
    return jnp.dot(left, right, precision=lax.Precision.HIGH, preferred_element_type=jnp.float32)


def contract_first(left, right):
    return lax.dot_general(
        left,
        right,
        (((0,), (0,)), ((), ())),
        precision=lax.Precision.HIGH,
        preferred_element_type=jnp.float32,
    )


def reduce_scatter_columns(partial, axis):
    index = lax.axis_index(axis)
    count = lax.axis_size(axis)
    current = partial
    bit = 1
    while bit < count:
        width = current.shape[1] // 2
        upper = (index // bit) % 2
        send = lax.dynamic_slice_in_dim(current, (1 - upper) * width, width, axis=1)
        keep = lax.dynamic_slice_in_dim(current, upper * width, width, axis=1)
        current = keep + swap(send, axis, bit)
        bit *= 2
    return current


def all_gather_columns(share, axis):
    index = lax.axis_index(axis)
    count = lax.axis_size(axis)
    current = share
    bit = count // 2
    while bit >= 1:
        other = swap(current, axis, bit)
        upper = (index // bit) % 2
        width = current.shape[1]
        joined = jnp.zeros((current.shape[0], 2 * width), current.dtype)
        joined = lax.dynamic_update_slice_in_dim(joined, current, upper * width, axis=1)
        current = lax.dynamic_update_slice_in_dim(joined, other, (1 - upper) * width, axis=1)
        bit //= 2
    return current


def gamma_over_aux(screened, densities):
    count = lax.axis_size("aux")
    index = lax.axis_index("aux")
    rows = densities.shape[0]

    def columns(block):
        start = jnp.clip(block, 0, count - 1) * rows
        return lax.dynamic_slice_in_dim(screened, start, rows, axis=1)

    gamma = product(columns(index), densities)
    from_left, from_right = densities, densities
    for step in range(count - 1):
        rightward = [(i, i + 1) for i in range(step, count - 1)]
        leftward = [(i + 1, i) for i in range(count - 1 - step)]
        from_left = lax.ppermute(from_left, "aux", rightward)
        from_right = lax.ppermute(from_right, "aux", leftward)
        gamma = gamma + product(columns(index - 1 - step), from_left)
        gamma = gamma + product(columns(index + 1 + step), from_right)
    return gamma


def reduce_over_aux(partial):
    count = lax.axis_size("aux")
    index = lax.axis_index("aux")
    rows = partial.shape[0] // count

    def block(owner):
        start = jnp.clip(owner, 0, count - 1) * rows
        return lax.dynamic_slice_in_dim(partial, start, rows, axis=0)

    to_right = jnp.zeros((rows, partial.shape[1]), partial.dtype)
    to_left = jnp.zeros((rows, partial.shape[1]), partial.dtype)
    for step in range(count - 1):
        rightward = [(i, i + 1) for i in range(min(step + 1, count - 1))]
        leftward = [(i + 1, i) for i in range(count - 2 - step, count - 1)]
        to_right = lax.ppermute(to_right + block(index + count - 1 - step), "aux", rightward)
        to_left = lax.ppermute(to_left + block(index - (count - 1) + step), "aux", leftward)
    return to_right + to_left + block(index)


def solve(right_side, transfer, diag_inverse, sub_factor):
    driving = product(diag_inverse, right_side)
    chain_length = lax.axis_size("aux")
    incoming = jnp.zeros_like(driving)
    for turn in range(chain_length - 1):
        value = driving if turn == 0 else product(transfer, incoming) + driving
        incoming = incoming + lax.ppermute(value, "aux", [(turn, turn + 1)])
    solved = product(transfer, incoming) + driving
    source = product(sub_factor.T, product(diag_inverse.T, solved))
    back_map = transfer.T
    arriving = jnp.zeros_like(driving)
    for turn in range(chain_length - 1):
        sender = chain_length - 1 - turn
        value = source if turn == 0 else product(back_map, arriving) + source
        arriving = arriving + lax.ppermute(value, "aux", [(sender, sender - 1)])
    return product(diag_inverse.T, solved - arriving)


SLICES = 2


def per_device(three_center, densities, screen_mask, diag_inverse, sub_factor):
    screened = screen_block(three_center, screen_mask)
    transfer = -product(diag_inverse, sub_factor)
    gamma_partial = gamma_over_aux(screened, densities)
    width = gamma_partial.shape[1] // SLICES
    results = []
    for part in range(SLICES):
        right_side = reduce_scatter_columns(gamma_partial[:, part * width:(part + 1) * width], "pair")
        coefficients = solve(right_side, transfer, diag_inverse, sub_factor)
        coeff_full = all_gather_columns(coefficients, "pair")
        partial = contract_first(screened, coeff_full)
        results.append(reduce_over_aux(partial))
    return jnp.concatenate(results, axis=1)


def solution(mesh):
    return jax.shard_map(
        per_device,
        mesh=mesh,
        in_specs=(
            P("aux", "pair"),
            P(("pair", "aux"), None),
            P("aux", "pair"),
            P("aux", None),
            P("aux", None),
        ),
        out_specs=P(("pair", "aux"), None),
        check_vma=False,
    )
```

```python
import jax
import jax.numpy as jnp
from jax import lax
from jax.sharding import PartitionSpec as P


def from_behind(array, axis, by):
    count = lax.axis_size(axis)
    pairs = [(i, i + by) for i in range(count) if 0 <= i + by < count]
    return lax.ppermute(array, axis, pairs)


def swap(array, axis, bit):
    count = lax.axis_size(axis)
    return lax.ppermute(array, axis, [(i, i ^ bit) for i in range(count)])


def screen_block(block, screen_mask):
    aux_blocks, pair_blocks = screen_mask.shape
    aux_size = block.shape[0] // aux_blocks
    pair_size = block.shape[1] // pair_blocks
    expanded = jnp.repeat(jnp.repeat(screen_mask.astype(jnp.float32), aux_size, 0), pair_size, 1)
    return block * expanded


def product(left, right):
    return jnp.dot(left, right, precision=lax.Precision.HIGH, preferred_element_type=jnp.float32)


def contract_first(left, right):
    return lax.dot_general(
        left,
        right,
        (((0,), (0,)), ((), ())),
        precision=lax.Precision.HIGH,
        preferred_element_type=jnp.float32,
    )


def reduce_scatter_columns(partial, axis):
    index = lax.axis_index(axis)
    count = lax.axis_size(axis)
    current = partial
    bit = 1
    while bit < count:
        width = current.shape[1] // 2
        low, high = current[:, :width], current[:, width:]
        upper = (index // bit) % 2 == 1
        send = jnp.where(upper, low, high)
        keep = jnp.where(upper, high, low)
        current = keep + swap(send, axis, bit)
        bit *= 2
    return current


def all_gather_columns(share, axis):
    index = lax.axis_index(axis)
    count = lax.axis_size(axis)
    current = share
    bit = count // 2
    while bit >= 1:
        other = swap(current, axis, bit)
        upper = (index // bit) % 2
        width = current.shape[1]
        joined = jnp.zeros((current.shape[0], 2 * width), current.dtype)
        joined = lax.dynamic_update_slice_in_dim(joined, current, upper * width, axis=1)
        current = lax.dynamic_update_slice_in_dim(joined, other, (1 - upper) * width, axis=1)
        bit //= 2
    return current


def gamma_over_aux(screened, densities):
    count = lax.axis_size("aux")
    index = lax.axis_index("aux")
    rows = densities.shape[0]

    def columns(block):
        start = jnp.clip(block, 0, count - 1) * rows
        return lax.dynamic_slice_in_dim(screened, start, rows, axis=1)

    gamma = product(columns(index), densities)
    from_left, from_right = densities, densities
    for step in range(count - 1):
        rightward = [(i, i + 1) for i in range(step, count - 1)]
        leftward = [(i + 1, i) for i in range(count - 1 - step)]
        from_left = lax.ppermute(from_left, "aux", rightward)
        from_right = lax.ppermute(from_right, "aux", leftward)
        gamma = gamma + product(columns(index - 1 - step), from_left)
        gamma = gamma + product(columns(index + 1 + step), from_right)
    return gamma


def reduce_over_aux(partial):
    count = lax.axis_size("aux")
    index = lax.axis_index("aux")
    rows = partial.shape[0] // count

    def block(owner):
        start = jnp.clip(owner, 0, count - 1) * rows
        return lax.dynamic_slice_in_dim(partial, start, rows, axis=0)

    to_right = jnp.zeros((rows, partial.shape[1]), partial.dtype)
    to_left = jnp.zeros((rows, partial.shape[1]), partial.dtype)
    for step in range(count - 1):
        rightward = [(i, i + 1) for i in range(min(step + 1, count - 1))]
        leftward = [(i + 1, i) for i in range(count - 2 - step, count - 1)]
        to_right = lax.ppermute(to_right + block(index + count - 1 - step), "aux", rightward)
        to_left = lax.ppermute(to_left + block(index - (count - 1) + step), "aux", leftward)
    return to_right + to_left + block(index)


def solve(right_side, transfer, diag_inverse, sub_factor):
    driving = product(diag_inverse, right_side)
    chain_length = lax.axis_size("aux")
    incoming = jnp.zeros_like(driving)
    for turn in range(chain_length - 1):
        value = driving if turn == 0 else product(transfer, incoming) + driving
        incoming = incoming + lax.ppermute(value, "aux", [(turn, turn + 1)])
    solved = product(transfer, incoming) + driving
    back_map = transfer.T
    source = -product(back_map, solved)
    arriving = jnp.zeros_like(driving)
    for turn in range(chain_length - 1):
        sender = chain_length - 1 - turn
        value = source if turn == 0 else product(back_map, arriving) + source
        arriving = arriving + lax.ppermute(value, "aux", [(sender, sender - 1)])
    return product(diag_inverse.T, solved - arriving)


SLICES = 2


def per_device(three_center, densities, screen_mask, diag_inverse, sub_factor):
    screened = screen_block(three_center, screen_mask)
    transfer = -product(diag_inverse, sub_factor)
    gamma_partial = gamma_over_aux(screened, densities)
    width = gamma_partial.shape[1] // SLICES
    results = []
    for part in range(SLICES):
        right_side = reduce_scatter_columns(gamma_partial[:, part * width:(part + 1) * width], "pair")
        coefficients = solve(right_side, transfer, diag_inverse, sub_factor)
        coeff_full = all_gather_columns(coefficients, "pair")
        partial = contract_first(screened, coeff_full)
        results.append(reduce_over_aux(partial))
    return jnp.concatenate(results, axis=1)


def solution(mesh):
    return jax.shard_map(
        per_device,
        mesh=mesh,
        in_specs=(
            P("aux", "pair"),
            P(("pair", "aux"), None),
            P("aux", "pair"),
            P("aux", None),
            P("aux", None),
        ),
        out_specs=P(("pair", "aux"), None),
        check_vma=False,
    )
```

```python
import jax
import jax.numpy as jnp
from jax import lax
from jax.sharding import PartitionSpec as P


def from_behind(array, axis, by):
    count = lax.axis_size(axis)
    pairs = [(i, i + by) for i in range(count) if 0 <= i + by < count]
    return lax.ppermute(array, axis, pairs)


def swap(array, axis, bit):
    count = lax.axis_size(axis)
    return lax.ppermute(array, axis, [(i, i ^ bit) for i in range(count)])


def screen_block(block, screen_mask):
    aux_blocks, pair_blocks = screen_mask.shape
    aux_size = block.shape[0] // aux_blocks
    pair_size = block.shape[1] // pair_blocks
    expanded = jnp.repeat(jnp.repeat(screen_mask.astype(jnp.float32), aux_size, 0), pair_size, 1)
    return block * expanded


def product(left, right):
    return jnp.dot(left, right, precision=lax.Precision.HIGH, preferred_element_type=jnp.float32)


def contract_first(left, right):
    return lax.dot_general(
        left,
        right,
        (((0,), (0,)), ((), ())),
        precision=lax.Precision.HIGH,
        preferred_element_type=jnp.float32,
    )


def reduce_scatter_columns(partial, axis):
    index = lax.axis_index(axis)
    count = lax.axis_size(axis)
    current = partial
    bit = 1
    while bit < count:
        width = current.shape[1] // 2
        low, high = current[:, :width], current[:, width:]
        upper = (index // bit) % 2 == 1
        send = jnp.where(upper, low, high)
        keep = jnp.where(upper, high, low)
        current = keep + swap(send, axis, bit)
        bit *= 2
    return current


def all_gather_columns(share, axis):
    index = lax.axis_index(axis)
    count = lax.axis_size(axis)
    current = share
    bit = count // 2
    while bit >= 1:
        other = swap(current, axis, bit)
        upper = (index // bit) % 2
        width = current.shape[1]
        joined = jnp.zeros((current.shape[0], 2 * width), current.dtype)
        joined = lax.dynamic_update_slice_in_dim(joined, current, upper * width, axis=1)
        current = lax.dynamic_update_slice_in_dim(joined, other, (1 - upper) * width, axis=1)
        bit //= 2
    return current


def gamma_over_aux(screened, densities):
    count = lax.axis_size("aux")
    index = lax.axis_index("aux")
    rows = densities.shape[0]

    def columns(block):
        start = jnp.clip(block, 0, count - 1) * rows
        return lax.dynamic_slice_in_dim(screened, start, rows, axis=1)

    gamma = product(columns(index), densities)
    from_left, from_right = densities, densities
    for step in range(count - 1):
        rightward = [(i, i + 1) for i in range(step, count - 1)]
        leftward = [(i + 1, i) for i in range(count - 1 - step)]
        from_left = lax.ppermute(from_left, "aux", rightward)
        from_right = lax.ppermute(from_right, "aux", leftward)
        both_columns = jnp.concatenate([columns(index - 1 - step), columns(index + 1 + step)], axis=1)
        gamma = gamma + product(both_columns, jnp.concatenate([from_left, from_right], axis=0))
    return gamma


def reduce_over_aux(partial):
    count = lax.axis_size("aux")
    index = lax.axis_index("aux")
    rows = partial.shape[0] // count

    def block(owner):
        start = jnp.clip(owner, 0, count - 1) * rows
        return lax.dynamic_slice_in_dim(partial, start, rows, axis=0)

    to_right = jnp.zeros((rows, partial.shape[1]), partial.dtype)
    to_left = jnp.zeros((rows, partial.shape[1]), partial.dtype)
    for step in range(count - 1):
        rightward = [(i, i + 1) for i in range(min(step + 1, count - 1))]
        leftward = [(i + 1, i) for i in range(count - 2 - step, count - 1)]
        to_right = lax.ppermute(to_right + block(index + count - 1 - step), "aux", rightward)
        to_left = lax.ppermute(to_left + block(index - (count - 1) + step), "aux", leftward)
    return to_right + to_left + block(index)


def solve(right_side, transfer, diag_inverse, sub_factor):
    driving = product(diag_inverse, right_side)
    chain_length = lax.axis_size("aux")
    incoming = jnp.zeros_like(driving)
    for turn in range(chain_length - 1):
        value = driving if turn == 0 else product(transfer, incoming) + driving
        incoming = incoming + lax.ppermute(value, "aux", [(turn, turn + 1)])
    solved = product(transfer, incoming) + driving
    back_map = transfer.T
    source = -product(back_map, solved)
    arriving = jnp.zeros_like(driving)
    for turn in range(chain_length - 1):
        sender = chain_length - 1 - turn
        value = source if turn == 0 else product(back_map, arriving) + source
        arriving = arriving + lax.ppermute(value, "aux", [(sender, sender - 1)])
    return product(diag_inverse.T, solved - arriving)


SLICES = 2


def per_device(three_center, densities, screen_mask, diag_inverse, sub_factor):
    screened = screen_block(three_center, screen_mask)
    transfer = -product(diag_inverse, sub_factor)
    gamma_partial = gamma_over_aux(screened, densities)
    width = gamma_partial.shape[1] // SLICES
    results = []
    for part in range(SLICES):
        right_side = reduce_scatter_columns(gamma_partial[:, part * width:(part + 1) * width], "pair")
        coefficients = solve(right_side, transfer, diag_inverse, sub_factor)
        coeff_full = all_gather_columns(coefficients, "pair")
        partial = contract_first(screened, coeff_full)
        results.append(reduce_over_aux(partial))
    return jnp.concatenate(results, axis=1)


def solution(mesh):
    return jax.shard_map(
        per_device,
        mesh=mesh,
        in_specs=(
            P("aux", "pair"),
            P(("pair", "aux"), None),
            P("aux", "pair"),
            P("aux", None),
            P("aux", None),
        ),
        out_specs=P(("pair", "aux"), None),
        check_vma=False,
    )
```
